32 devices in a mesh: groups: 2 (over y), tensor: 16 (over z, x, core), dp: 1.
Axes of the slice: x: 2, y: 2, z: 4, core: 2. Of those that a mesh axis runs over, the one named last changes fastest.
Arguments:
- x_first: bfloat16 [768, 8192], P(('groups', 'dp'), 'tensor'), parts along dimension 0, may hold values from -6 to 6
- target_first: bfloat16 [768, 8192], P(('groups', 'dp'), 'tensor'), parts along dimension 0, may hold values from -6 to 6
- x_second: bfloat16 [768, 8192], P(('groups', 'dp'), 'tensor'), parts along dimension 0, may hold values from -6 to 6
- target_second: bfloat16 [768, 8192], P(('groups', 'dp'), 'tensor'), parts along dimension 0, may hold values from -6 to 6
- frozen_weight_pairs: bfloat16 [4096, 16384], P(None, 'tensor'), may hold values from -0.0625 to 0.0625
- right_factor: float32 [256, 64, 64], P(('groups', 'tensor')), parts along dimension 0, may hold values from -0.75 to 0.75
- left_factor: float32 [256, 128, 64], P(('groups', 'tensor')), parts along dimension 0, may hold values from -0.5 to 0.5
Outputs:
- output: bfloat16 [768, 8192], P(('groups', 'dp'), 'tensor'), parts along dimension 0
- right_final: float32 [256, 64, 64], P(('groups', 'tensor')), parts along dimension 0
- left_final: float32 [256, 128, 64], P(('groups', 'tensor')), parts along dimension 0
The draws below stay inside these ranges and needn't reach their ends.
There are 2 independent parts, one for each index of `groups`. The reference program is written for one: setup_inputs(seed, part) draws one part's arguments, and reference() takes and returns one part's arrays. A program takes and returns all parts, laid end to end along the dimension named above; an argument that names none is the same for every part. Nothing has to cross between parts.
All inputs are finite; a program needn't handle non-finite values.
Results may differ from the reference program's by a relative error of at most 0.018.
Values may be sent and summed in bfloat16 or wider, within the bound.
A program may use at most 128 MiB of HBM per device.

```python
import jax
import jax.numpy as jnp
from jax import lax

D = 8192
NB = 128
BS = 64
TOKENS = 384


def levels(key, shape, cuts, smallest, high):
    def one(axis_at, parts):
        draws = jax.random.uniform(jax.random.fold_in(jax.random.fold_in(key, 6), axis_at), (parts,), jnp.float32, smallest / len(cuts), high / len(cuts))
        return jnp.repeat(jnp.exp(draws), shape[axis_at] // parts).reshape((-1,) + (1,) * (len(shape) - axis_at - 1))

    loudness = one(*cuts[0])
    for cut in cuts[1:]:
        loudness = loudness * one(*cut)
    return loudness


def bell_draw(stream_key, extent, scale, reach, cuts=(), kind=jnp.bfloat16):
    values = jax.random.normal(stream_key, extent, jnp.float32) * scale
    if len(cuts) > 0:
        values = levels(stream_key, extent, cuts, -0.22, 0.18) * values
    return jnp.clip(values, min=-reach, max=reach).astype(kind)


def setup_inputs(seed: int = 0, part: int = 0) -> dict:
    streams_of = jax.random.split(jax.random.key(seed), 8)
    part_splits = jax.random.split(jax.random.fold_in(streams_of[7], part), 8)
    x_first = bell_draw(part_splits[0], (TOKENS, D), 1.0, 6.0, ((1, 16),))
    target_first = bell_draw(part_splits[1], (TOKENS, D), 1.0, 6.0, ((1, 16),))
    x_second = bell_draw(part_splits[2], (TOKENS, D), 1.0, 6.0, ((1, 16),))
    target_second = bell_draw(part_splits[3], (TOKENS, D), 1.0, 6.0, ((1, 16),))
    frozen_weight_pairs = bell_draw(streams_of[4], (D // 2, 2 * D), D ** -0.5, 0.0625, ((1, 16),))
    right_factor = bell_draw(part_splits[5], (NB, BS, BS), BS ** -0.5, 0.75, ((0, 16),), jnp.float32)
    left_factor = bell_draw(part_splits[6], (NB, NB, BS), NB ** -0.5, 0.5, ((0, 16),), jnp.float32)
    return dict(x_first=x_first, target_first=target_first, x_second=x_second, target_second=target_second, frozen_weight_pairs=frozen_weight_pairs, right_factor=right_factor, left_factor=left_factor)


exact_precision = lax.Precision.HIGHEST


def to_half(values):
    return lax.optimization_barrier(values.astype(jnp.bfloat16))


def unpack_weight(stored, block_size):
    half_rows = stored.shape[0]
    grid_cols = stored.shape[1] // (2 * block_size)
    split = stored.reshape(half_rows, grid_cols, 2, block_size).transpose(0, 2, 1, 3)
    return split.reshape(2 * half_rows, grid_cols * block_size)


def adapter_step(inputs, target, weight, right_factor, left_factor):
    token_count = inputs.shape[0]
    mesh_row_count = left_factor.shape[1]
    block_size = right_factor.shape[1]
    sub_count = mesh_row_count // block_size
    base_out = jnp.dot(inputs, weight, preferred_element_type=jnp.float32)
    upper_right_half = to_half(right_factor).astype(jnp.float32)
    left_half = to_half(left_factor).astype(jnp.float32).reshape(block_size, sub_count, mesh_row_count, block_size)
    input_mesh_grid = inputs.astype(jnp.float32).reshape(token_count, mesh_row_count, block_size)
    hidden = to_half(jnp.einsum("tic,icd->tid", input_mesh_grid, upper_right_half, precision=exact_precision)).astype(jnp.float32)
    mixed_out = to_half(jnp.einsum("tij,jhik->thkj", hidden, left_half, precision=exact_precision)).astype(jnp.float32)
    mixed_out = mixed_out.reshape(token_count, mesh_row_count * block_size)
    offset = to_half(base_out - target.astype(jnp.float32)).astype(jnp.float32)
    residual_err = to_half(offset + mixed_out).astype(jnp.float32)
    residual_err = residual_err.reshape(token_count, sub_count, block_size, block_size)
    left_grad = jnp.einsum("tij,thkj->jhik", hidden, residual_err, precision=exact_precision)
    left_grad = left_grad.reshape(mesh_row_count, mesh_row_count, block_size)
    back_terms = to_half(jnp.einsum("thkj,jhik->thij", residual_err, left_half, precision=exact_precision)).astype(jnp.float32)
    hidden_gradient = jnp.sum(back_terms, axis=1)
    right_grad = jnp.einsum("tic,tid->icd", input_mesh_grid, hidden_gradient, precision=exact_precision)
    return base_out + mixed_out, right_grad, left_grad


def reference(x_first, target_first, x_second, target_second, frozen_weight_pairs, right_factor, left_factor):
    step_size = 1.0 / TOKENS
    weight = unpack_weight(frozen_weight_pairs, right_factor.shape[1])
    unused, right_grad, left_grad = adapter_step(x_first, target_first, weight, right_factor, left_factor)
    right_now = right_factor - step_size * right_grad
    left_now = left_factor - step_size * left_grad
    result, right_grad, left_grad = adapter_step(x_second, target_second, weight, right_now, left_now)
    right_now = right_now - step_size * right_grad
    left_now = left_now - step_size * left_grad
    return result.astype(jnp.bfloat16), right_now, left_now
```

```python
import functools

import jax
import jax.numpy as jnp
from jax import lax
from jax.experimental import pallas as pl
from jax.experimental.pallas import tpu as pltpu
from jax.sharding import PartitionSpec as P

MESH = pl.DeviceIdType.MESH
BF = jnp.bfloat16
F32 = jnp.float32
LANES = (((1,), (1,)), ((), ()))

exact_precision = lax.Precision.HIGHEST


def toward_blocks(buffer_rows):
    return lax.all_to_all(buffer_rows, "tensor", split_axis=0, concat_axis=1, tiled=True)


def toward_rows(buffer_blocks):
    return lax.all_to_all(buffer_blocks, "tensor", split_axis=1, concat_axis=0, tiled=True)


def rows_direct(buffer_rows):
    return lax.all_to_all(buffer_rows, "tensor", split_axis=0, concat_axis=1, tiled=True)


def blocks_direct(buffer_blocks):
    return lax.all_to_all(buffer_blocks, "tensor", split_axis=1, concat_axis=0, tiled=True)


def make_masks(rows_local, mesh_row_count, block_size):
    sub_count = mesh_row_count // block_size
    own_index = lax.axis_index("tensor") * rows_local + jnp.arange(rows_local, dtype=jnp.int32)
    positions = jnp.arange(sub_count, dtype=jnp.int32)
    block_mask = (positions[None, :] == (own_index % sub_count)[:, None]).astype(jnp.bfloat16)
    row_mask = (positions[:, None] == (own_index // block_size)[None, :]).astype(jnp.bfloat16)
    return (block_mask, row_mask)


def spread_rows(values, row_mask):
    block_size, rows_local, token_count = values.shape
    sub_count = row_mask.shape[0]
    spread = values[:, None, :, :] * row_mask[None, :, :, None]
    return spread.reshape(block_size * sub_count, rows_local, token_count)


def pick_block(received, block_mask):
    rows_local, mesh_row_count, token_count = received.shape
    sub_count = block_mask.shape[1]
    split = received.reshape(rows_local, sub_count, mesh_row_count // sub_count, token_count)
    return jnp.sum(split * block_mask[:, :, None, None], axis=1)


def spread_block(values, block_mask):
    rows_local, block_size, token_count = values.shape
    sub_count = block_mask.shape[1]
    spread = values[:, None, :, :] * block_mask[:, :, None, None]
    return spread.reshape(rows_local, sub_count * block_size, token_count)


def pick_rows(received, row_mask):
    mesh_row_count, rows_local, token_count = received.shape
    sub_count = row_mask.shape[0]
    split = received.reshape(mesh_row_count // sub_count, sub_count, rows_local, token_count)
    return jnp.sum(split * row_mask[None, :, :, None], axis=1)


def paired_product(segment, weight, block_size):
    token_count, width = segment.shape
    grid_local = weight.shape[1] // (2 * block_size)
    weight_rows = weight
    weight_rows = weight_rows.reshape(width // 2, grid_local, 2, block_size)
    pairs = segment.reshape(token_count, width // 2, 2)
    partial_value = jnp.einsum(
        "trs,rgsc->tgc", pairs, weight_rows, preferred_element_type=jnp.float32
    )
    return partial_value.reshape(token_count, grid_local * block_size)


def base_product(x_local, weight, block_size):
    return paired_product(lax.all_gather(x_local, "tensor", axis=1, tiled=True), weight, block_size)


def rows_to_block_side(values, masks_pair):
    return pick_block(rows_direct(spread_rows(values, masks_pair[1])), masks_pair[0])


def block_to_row_side(values, masks_pair):
    return pick_rows(blocks_direct(spread_block(values, masks_pair[0])), masks_pair[1])


def one_step(x_local, target, base_out, right_factor, left_factor, masks_pair, step_size):
    token_count = x_local.shape[0]
    rows_local = right_factor.shape[0]
    block_size = right_factor.shape[1]
    sub_count = left_factor.shape[1] // block_size
    upper_right_half = right_factor.astype(jnp.bfloat16)
    left_half = left_factor.astype(jnp.bfloat16)
    input_mesh_grid = x_local.reshape(token_count, rows_local, block_size)
    base_rows = base_out.reshape(token_count, rows_local, block_size).transpose(2, 1, 0)
    target_rows = (
        target.reshape(token_count, rows_local, block_size).transpose(2, 1, 0).astype(jnp.float32)
    )
    offset = (base_rows - target_rows).astype(jnp.bfloat16)
    hidden = jnp.einsum(
        "ves,esl->lev", input_mesh_grid, upper_right_half, preferred_element_type=jnp.float32
    ).astype(jnp.bfloat16)
    gathered = toward_blocks(jnp.repeat(hidden, sub_count, axis=0))
    mixed_out = jnp.einsum(
        "sit,sik->skt", gathered, left_half, preferred_element_type=jnp.float32
    ).astype(jnp.bfloat16)
    output_rows = None
    mixed_rows = block_to_row_side(mixed_out, masks_pair)
    output_rows = base_rows + mixed_rows.astype(jnp.float32)
    error_rows = (offset.astype(jnp.float32) + mixed_rows.astype(jnp.float32)).astype(jnp.bfloat16)
    error_blocks = rows_to_block_side(error_rows, masks_pair)
    left_grad = jnp.einsum(
        "sit,skt->sik", gathered, error_blocks, preferred_element_type=jnp.float32
    )
    back_terms = jnp.einsum(
        "skt,sik->sit", error_blocks, left_half, preferred_element_type=jnp.float32
    ).astype(jnp.bfloat16)
    returned = toward_rows(back_terms)
    hidden_gradient = jnp.sum(
        returned.reshape(block_size, sub_count, rows_local, token_count).astype(jnp.float32), axis=1
    )
    right_grad = jnp.einsum(
        "wfm,sfw->fms",
        input_mesh_grid.astype(jnp.float32),
        hidden_gradient,
        precision=exact_precision,
    )
    right_grad, left_grad = lax.psum((right_grad, left_grad), "dp")
    return (output_rows, right_factor - step_size * right_grad, left_factor - step_size * left_grad)


def shards(
    x_first, target_first, x_second, target_second, frozen_weight_pairs, right_factor, left_factor
):
    rows_local = right_factor.shape[0]
    block_size = right_factor.shape[1]
    token_count = x_first.shape[0]
    masks_pair = make_masks(rows_local, left_factor.shape[1], block_size)
    step_size = 1.0 / (token_count * lax.axis_size("dp"))
    base_first = base_product(x_first, frozen_weight_pairs, block_size)
    unused, right_now, left_now = one_step(
        x_first, target_first, base_first, right_factor, left_factor, masks_pair, step_size
    )
    base_second = base_product(x_second, frozen_weight_pairs, block_size)
    output_rows, right_now, left_now = one_step(
        x_second, target_second, base_second, right_now, left_now, masks_pair, step_size
    )
    result = (
        output_rows.transpose(2, 1, 0)
        .reshape(token_count, rows_local * block_size)
        .astype(jnp.bfloat16)
    )
    return (result, right_now, left_now)


Z_COUNT, DEVICES, ROWS, COLS = 4, 16, 8, 4
PIECES = ((0, 0, 384), (1, 0, 256), (1, 256, 128))
RIGHT_IN, RIGHT_BACK, OFFSET, MIXED = 0, 1, 2, 2 + len(PIECES)
KINDS = 2 + 2 * len(PIECES)


def adapter_kernel(
    step_size, x1, t1, x2, t2, weight, right_in, left_in, out, left_out, right_out,
    w, wd, xg, acc, base, rgrad, rhalf, lhalf, lturn, hid, hgrad, mixed, right_send, right_recv,
    back_send, back_recv, off_send, off_recv, mix_send, mix_recv,
    w_sem, ag_send, ag_recv, a2a_send, a2a_recv,
):
    tokens, width = x1.shape
    half = width // 2
    me = lax.axis_index("tensor")
    z, x, core = me // 4, lax.rem(me // 2, 2), lax.rem(me, 2)
    x_peer = z * 4 + (1 - x) * 2 + core
    core_peer = z * 4 + x * 2 + (1 - core)

    w_copy = pltpu.make_async_copy(weight, w, w_sem)
    w_copy.start()

    barrier = pltpu.get_barrier_semaphore()

    @pl.loop(1, DEVICES)
    def _(n):
        pl.semaphore_signal(
            barrier, inc=1, device_id={"tensor": lax.rem(me + n, DEVICES)}, device_id_type=MESH
        )

    row_id = lax.broadcasted_iota(jnp.int32, (width, width), 0)
    col_id = lax.broadcasted_iota(jnp.int32, (width, width), 1)
    split = jnp.where(row_id == 2 * lax.rem(col_id, half) + col_id // half, 1.0, 0.0).astype(BF)
    xg[0, me] = jnp.dot(x1[...], split, preferred_element_type=F32).astype(BF)

    pl.semaphore_wait(barrier, DEVICES - 1)

    def exchange(kind, source, target, peer, cut):
        return pltpu.make_async_remote_copy(
            src_ref=source.at[peer, :, cut],
            dst_ref=target.at[me, :, cut],
            send_sem=a2a_send.at[kind, peer],
            recv_sem=a2a_recv.at[kind, me],
            device_id={"tensor": peer},
            device_id_type=MESH,
        )

    def landed(kind, target, peer, cut):
        return pltpu.make_async_remote_copy(
            src_ref=target.at[peer, :, cut],
            dst_ref=target.at[peer, :, cut],
            send_sem=a2a_send.at[kind, peer],
            recv_sem=a2a_recv.at[kind, peer],
            device_id={"tensor": peer},
            device_id_type=MESH,
        )

    def send_all(kind, source, target, cut):
        @pl.loop(1, DEVICES)
        def _(n):
            exchange(kind, source, target, lax.rem(me + n, DEVICES), cut).start()

        target[me, :, cut] = source[me, :, cut]

    def wait_all(kind, target, cut):
        @pl.loop(1, DEVICES)
        def _(n):
            landed(kind, target, lax.rem(me + n, DEVICES), cut).wait_recv()

    def sent_all(kind, source, target, cut):
        @pl.loop(1, DEVICES)
        def _(n):
            exchange(kind, source, target, lax.rem(me + n, DEVICES), cut).wait_send()

    def span(piece):
        return slice(PIECES[piece][1], PIECES[piece][1] + PIECES[piece][2])

    def hop(piece, chunk, direction, peer):
        b = PIECES[piece][0]
        return pltpu.make_async_remote_copy(
            src_ref=xg.at[b, chunk, span(piece)],
            dst_ref=xg.at[b, chunk, span(piece)],
            send_sem=ag_send.at[piece, chunk, direction],
            recv_sem=ag_recv.at[piece, chunk],
            device_id={"tensor": peer},
            device_id_type=MESH,
        )

    def z_order(k):
        high = z // 2
        mirrored = z * (1 - high) + (3 - z) * high
        order = k + (1 - k // 2) * mirrored * (1 - 2 * k)
        return order * (1 - high) + (3 - order) * high

    def along_z(piece, source_z, act):
        chunk = source_z * 4 + x * 2 + core

        @pl.when((source_z <= z) & (z < Z_COUNT - 1))
        def _():
            act(hop(piece, chunk, 0, me + 4))

        @pl.when((source_z >= z) & (z > 0))
        def _():
            act(hop(piece, chunk, 1, me - 4))

    def across(piece, source_z, act):
        chunk = source_z * 4 + x * 2 + core
        act(hop(piece, chunk, 2, x_peer))
        act(hop(piece, chunk, 3, core_peer))

    def start(copy):
        copy.start()

    def apply_base(piece, chunk):
        b, cut = PIECES[piece][0], span(piece)
        acc[cut, :] += jnp.dot(xg[b, chunk, cut, :], wd[chunk], preferred_element_type=F32)

    def apply_hidden(piece, chunk):
        b, cut = PIECES[piece][0], span(piece)
        value = lax.dot_general(
            rhalf[chunk], xg[b, chunk, cut, :], LANES, preferred_element_type=F32
        )
        for d in range(COLS):
            hid[d, pl.ds(pl.multiple_of(chunk * ROWS, ROWS), ROWS), cut] = value[
                d * ROWS : (d + 1) * ROWS
            ]

    def gather(piece, first, last, with_hidden):
        ahead = piece + 1 if piece + 1 < len(PIECES) else None

        def use(chunk):
            apply_base(piece, chunk)
            if with_hidden:
                apply_hidden(piece, chunk)

        def body(k, carry):
            source_z = z_order(k)

            def own_side(m, inner_carry):
                chunk = source_z * 4 + x * 2 + core + m * (1 - 2 * core)

                @pl.when(m > 0)
                def _():
                    hop(piece, chunk, 3, core_peer).wait_recv()

                use(chunk)
                return inner_carry

            def other_side(m, inner_carry):
                chunk = source_z * 4 + (1 - x) * 2 + core + m * (1 - 2 * core)
                hop(piece, chunk, 3, core_peer).wait_recv()

                @pl.when(m == 0)
                def _():
                    hop(piece, chunk, 3, core_peer).start()

                use(chunk)
                return inner_carry

            lax.fori_loop(0, 2, own_side, 0)

            @pl.when(k < 3)
            def _():
                next_z = z_order(k + 1)
                hop(piece, next_z * 4 + x * 2 + core, 3, core_peer).wait_recv()
                along_z(piece, next_z, start)
                across(piece, next_z, start)

            if ahead is not None:

                @pl.when(k == 2)
                def _():
                    along_z(ahead, z, start)

                @pl.when(k == 3)
                def _():
                    across(ahead, z, start)

            lax.fori_loop(0, 2, other_side, 0)
            return carry

        lax.fori_loop(first, last, body, 0)

    def sent_gather(piece):
        @pl.loop(0, Z_COUNT)
        def _(source_z):
            along_z(piece, source_z, lambda copy: copy.wait_send())
            across(piece, source_z, lambda copy: copy.wait_send())
            hop(piece, source_z * 4 + (1 - x) * 2 + core, 3, core_peer).wait_send()

    def clear(piece):
        acc[span(piece), :] = jnp.zeros((PIECES[piece][2], width), F32)

    def finish_base(piece, target):
        b, cut, count = PIECES[piece][0], span(piece), PIECES[piece][2]
        value = acc[cut, :]
        if b == 1:
            base[cut, :] = value
        offset = (value - target[cut, :].astype(F32)).astype(BF)
        turned = lax.dot_general(turn, offset, LANES, preferred_element_type=F32)
        off_send[b, :, :, cut] = turned.astype(BF).reshape(DEVICES, COLS * ROWS, count)
        send_all(OFFSET + piece, off_send.at[b], off_recv.at[b], cut)

    def take_left(ref):
        for d in range(COLS):
            pair = jnp.concatenate([ref[2 * d], ref[2 * d + 1]], axis=0)
            lturn[d] = pair.astype(BF)
            lhalf[d] = pair.T.astype(BF)

    def mix(piece):
        cut = span(piece)
        for d in range(COLS):
            mixed[d, :, cut] = (
                jnp.dot(lturn[d], hid[d, :, cut].astype(BF), preferred_element_type=F32)
                .astype(BF)
                .astype(F32)
            )

    def send_mixed(piece):
        cut, count = span(piece), PIECES[piece][2]
        stacked = jnp.stack(
            [mixed[d, :, cut].reshape(DEVICES, ROWS, count) for d in range(COLS)], axis=1
        )
        mix_send[:, :, cut] = stacked.reshape(DEVICES, COLS * ROWS, count).astype(BF)
        send_all(MIXED + piece, mix_send, mix_recv, cut)

    block_row = lax.broadcasted_iota(jnp.int32, (COLS * ROWS, width), 0)
    block_col = lax.broadcasted_iota(jnp.int32, (COLS * ROWS, width), 1)
    on_block = lax.rem(block_row, ROWS) == lax.rem(block_col, half) // (half // ROWS)

    def backward(piece):
        b, cut, count = PIECES[piece][0], span(piece), PIECES[piece][2]
        wait_all(OFFSET + piece, off_recv.at[b], cut)
        received = off_recv[b, :, :, cut].astype(F32).reshape(DEVICES, COLS, ROWS, count)
        for d in range(COLS):
            offset = received[:, d].reshape(DEVICES * ROWS, count)
            error = (offset + mixed[d, :, cut]).astype(BF)
            hgrad[d, :, cut] = jnp.dot(lhalf[d], error, preferred_element_type=F32)
            grad = step_size * lax.dot_general(
                error, hid[d, :, cut].astype(BF), LANES, preferred_element_type=F32
            )
            left_out[2 * d] = left_out[2 * d] - grad[:64]
            left_out[2 * d + 1] = left_out[2 * d + 1] - grad[64:]

        @pl.loop(0, DEVICES)
        def _(chunk):
            rows = pl.ds(pl.multiple_of(chunk * ROWS, ROWS), ROWS)
            left = jnp.concatenate([hgrad[d, rows, cut] for d in range(COLS)], axis=0).astype(BF)
            grad = jnp.dot(left, xg[b, chunk, cut, :], preferred_element_type=F32)
            rgrad[chunk] = rgrad[chunk] + jnp.where(on_block, grad, 0.0)

    small_lane = lax.broadcasted_iota(jnp.int32, (COLS * ROWS, 128), 1)

    def take_right():
        @pl.loop(0, DEVICES)
        def _(chunk):
            value = right_recv[chunk].astype(F32)
            turned = pltpu.roll(value, 64, 1)
            even = jnp.where(small_lane < 64, value, turned)
            odd = jnp.where(small_lane < 64, turned, value)
            full = jnp.where(on_block, jnp.concatenate([even, even, odd, odd], axis=1), 0.0)
            rhalf[chunk] = (full - step_size * rgrad[chunk]).astype(BF)

    def give_output(piece):
        cut, count = span(piece), PIECES[piece][2]
        wait_all(MIXED + piece, mix_recv, cut)
        rows_in = mix_recv[:, :, cut].reshape(DEVICES * COLS * ROWS, count).astype(F32)
        mixed_rows = jnp.dot(rows_in.T.astype(BF), turn, preferred_element_type=F32)
        out[cut, :] = (base[cut, :] + mixed_rows).astype(BF)

    along_z(0, z, start)
    across(0, z, start)

    block_id = lax.broadcasted_iota(jnp.int32, (64, 128), 0)
    lane_id = lax.broadcasted_iota(jnp.int32, (64, 128), 1)
    own_lane = block_id == 2 * lax.rem(lane_id, 32) + lane_id // 64
    pairs = jnp.where(own_lane, 1.0, 0.0).astype(BF)
    one_pair = jnp.where(own_lane & (lax.rem(lane_id, 64) < 32), 1.0, 0.0).astype(BF)
    spread = [
        jnp.dot(right_in[i].T.astype(BF), pairs, preferred_element_type=F32) for i in range(ROWS)
    ]
    right_send[...] = (
        jnp.stack(spread, axis=1).reshape(DEVICES, COLS * ROWS, 128).astype(BF)
    )
    lanes = slice(0, 128)
    send_all(RIGHT_IN, right_send, right_recv, lanes)

    xg[1, me] = jnp.dot(x2[...], split, preferred_element_type=F32).astype(BF)
    turn = jnp.where(
        col_id == lax.rem(row_id, ROWS) * (width // ROWS) + row_id // ROWS, 1.0, 0.0
    ).astype(BF)
    rgrad[...] = jnp.zeros_like(rgrad)
    left_out[...] = left_in[...]
    take_left(left_in)
    clear(0)
    w_copy.wait()
    low = lax.broadcasted_iota(jnp.int32, (half, 128), 1) < 64

    @pl.loop(0, DEVICES)
    def _(chunk):
        rows = pl.ds(pl.multiple_of(chunk * half, half), half)
        for n in range(width // 128):
            first = w[rows, 256 * n : 256 * n + 128]
            second = w[rows, 256 * n + 128 : 256 * n + 256]
            lanes_n = slice(128 * n, 128 * n + 128)
            wd[chunk, :half, lanes_n] = jnp.concatenate([first[:, :64], second[:, :64]], axis=1)
            wd[chunk, half:, lanes_n] = jnp.concatenate([first[:, 64:], second[:, 64:]], axis=1)

    wait_all(RIGHT_IN, right_recv, lanes)
    take_right()

    gather(0, 0, 4, True)
    finish_base(0, t1)
    clear(1)
    clear(2)
    mix(0)
    gather(1, 0, 2, False)
    backward(0)
    take_left(left_out)
    take_right()

    def early(m, carry):
        apply_hidden(1, z_order(m // 4) * 4 + lax.rem(m, 4))
        return carry

    lax.fori_loop(0, 8, early, 0)
    gather(1, 2, 4, True)
    finish_base(1, t2)
    mix(1)
    send_mixed(1)
    gather(2, 0, 4, True)
    finish_base(2, t2)
    mix(2)
    send_mixed(2)
    backward(1)
    give_output(1)
    backward(2)

    @pl.loop(0, DEVICES)
    def _(chunk):
        value = rgrad[chunk]
        folded = []
        for s in range(2):
            part = value[:, s * half : s * half + 128] + value[:, s * half + 128 : (s + 1) * half]
            part = part + pltpu.roll(part, 64, 1)
            folded.append(part + pltpu.roll(part, 32, 1))
        back_send[chunk] = jnp.where(small_lane < 64, folded[0], folded[1]).astype(BF)

    send_all(RIGHT_BACK, back_send, back_recv, lanes)
    give_output(2)
    wait_all(RIGHT_BACK, back_recv, lanes)
    returned = back_recv[...].astype(F32).reshape(DEVICES * COLS, ROWS, 128)
    for i in range(ROWS):
        grad = lax.dot_general(
            one_pair, returned[:, i, :].astype(BF), LANES, preferred_element_type=F32
        )
        right_out[i] = right_in[i] - step_size * grad

    for piece in range(len(PIECES)):
        sent_gather(piece)
        b = PIECES[piece][0]
        sent_all(OFFSET + piece, off_send.at[b], off_recv.at[b], span(piece))
        if b == 1:
            sent_all(MIXED + piece, mix_send, mix_recv, span(piece))
    sent_all(RIGHT_IN, right_send, right_recv, lanes)
    sent_all(RIGHT_BACK, back_send, back_recv, lanes)


def hand_over(out, left, right, out_to, left_to, right_to, sems):
    copies = [
        pltpu.make_async_copy(source, target, sems.at[n])
        for n, (source, target) in enumerate(((out, out_to), (left, left_to), (right, right_to)))
    ]
    for copy in copies:
        copy.start()
    for copy in copies:
        copy.wait()


def fused_shards(
    x_first, target_first, x_second, target_second, frozen_weight_pairs, right_factor, left_factor
):
    tokens, width = x_first.shape
    step_size = 1.0 / tokens
    left_turned = jnp.swapaxes(left_factor, 1, 2)
    vmem = pl.BlockSpec(memory_space=pltpu.VMEM)
    slab = (DEVICES, COLS * ROWS, tokens)
    small = pltpu.VMEM((DEVICES, COLS * ROWS, 128), BF)
    cols = pltpu.VMEM((COLS, DEVICES * ROWS, tokens), F32)
    square = pltpu.VMEM((COLS, 128, 128), BF)
    out, left_now, right_now = pl.pallas_call(
        functools.partial(adapter_kernel, step_size),
        out_shape=(
            jax.ShapeDtypeStruct((tokens, width), BF),
            jax.ShapeDtypeStruct(left_turned.shape, F32),
            jax.ShapeDtypeStruct(right_factor.shape, F32),
        ),
        in_specs=[vmem] * 4 + [pl.BlockSpec(memory_space=pl.ANY)] + [vmem] * 2,
        out_specs=(vmem, vmem, vmem),
        scratch_shapes=[
            pltpu.VMEM(frozen_weight_pairs.shape, BF),
            pltpu.VMEM((DEVICES, width, width), BF),
            pltpu.VMEM((2, DEVICES, tokens, width), BF),
            pltpu.VMEM((tokens, width), F32),
            pltpu.VMEM((tokens, width), F32),
            pltpu.VMEM((DEVICES, COLS * ROWS, width), F32),
            pltpu.VMEM((DEVICES, COLS * ROWS, width), BF),
            square,
            square,
            cols,
            cols,
            cols,
            small,
            small,
            small,
            small,
            pltpu.VMEM((2,) + slab, BF),
            pltpu.VMEM((2,) + slab, BF),
            pltpu.VMEM(slab, BF),
            pltpu.VMEM(slab, BF),
            pltpu.SemaphoreType.DMA,
            pltpu.SemaphoreType.DMA((len(PIECES), DEVICES, 4)),
            pltpu.SemaphoreType.DMA((len(PIECES), DEVICES)),
            pltpu.SemaphoreType.DMA((KINDS, DEVICES)),
            pltpu.SemaphoreType.DMA((KINDS, DEVICES)),
        ],
        compiler_params=pltpu.CompilerParams(
            collective_id=0, has_side_effects=True, vmem_limit_bytes=60 * 1024 * 1024
        ),
        name="adapter",
    )(
        x_first, target_first, x_second, target_second, frozen_weight_pairs, right_factor, left_turned
    )
    anywhere = pl.BlockSpec(memory_space=pl.ANY)
    results = (out, left_now, right_now)
    out, left_now, right_now = pl.pallas_call(
        hand_over,
        out_shape=tuple(jax.ShapeDtypeStruct(a.shape, a.dtype) for a in results),
        in_specs=[anywhere] * 3,
        out_specs=(anywhere,) * 3,
        scratch_shapes=[pltpu.SemaphoreType.DMA((3,))],
        name="hand_over",
    )(*results)
    return (out, right_now, jnp.swapaxes(left_now, 1, 2))


def solution(mesh):
    fused = mesh.shape["tensor"] == DEVICES and mesh.shape["dp"] == 1
    body = fused_shards if fused else shards
    return jax.shard_map(
        body,
        mesh=mesh,
        in_specs=(
            P(("groups", "dp"), "tensor"),
            P(("groups", "dp"), "tensor"),
            P(("groups", "dp"), "tensor"),
            P(("groups", "dp"), "tensor"),
            P(None, "tensor"),
            P(("groups", "tensor"), None, None),
            P(("groups", "tensor"), None, None),
        ),
        out_specs=(
            P(("groups", "dp"), "tensor"),
            P(("groups", "tensor"), None, None),
            P(("groups", "tensor"), None, None),
        ),
        check_vma=False,
    )
```

```python
import functools

import jax
import jax.numpy as jnp
from jax import lax
from jax.experimental import pallas as pl
from jax.experimental.pallas import tpu as pltpu
from jax.sharding import PartitionSpec as P

MESH = pl.DeviceIdType.MESH
BF = jnp.bfloat16
F32 = jnp.float32
LANES = (((1,), (1,)), ((), ()))

exact_precision = lax.Precision.HIGHEST


def toward_blocks(buffer_rows):
    return lax.all_to_all(buffer_rows, "tensor", split_axis=0, concat_axis=1, tiled=True)


def toward_rows(buffer_blocks):
    return lax.all_to_all(buffer_blocks, "tensor", split_axis=1, concat_axis=0, tiled=True)


def rows_direct(buffer_rows):
    return lax.all_to_all(buffer_rows, "tensor", split_axis=0, concat_axis=1, tiled=True)


def blocks_direct(buffer_blocks):
    return lax.all_to_all(buffer_blocks, "tensor", split_axis=1, concat_axis=0, tiled=True)


def make_masks(rows_local, mesh_row_count, block_size):
    sub_count = mesh_row_count // block_size
    own_index = lax.axis_index("tensor") * rows_local + jnp.arange(rows_local, dtype=jnp.int32)
    positions = jnp.arange(sub_count, dtype=jnp.int32)
    block_mask = (positions[None, :] == (own_index % sub_count)[:, None]).astype(jnp.bfloat16)
    row_mask = (positions[:, None] == (own_index // block_size)[None, :]).astype(jnp.bfloat16)
    return (block_mask, row_mask)


def spread_rows(values, row_mask):
    block_size, rows_local, token_count = values.shape
    sub_count = row_mask.shape[0]
    spread = values[:, None, :, :] * row_mask[None, :, :, None]
    return spread.reshape(block_size * sub_count, rows_local, token_count)


def pick_block(received, block_mask):
    rows_local, mesh_row_count, token_count = received.shape
    sub_count = block_mask.shape[1]
    split = received.reshape(rows_local, sub_count, mesh_row_count // sub_count, token_count)
    return jnp.sum(split * block_mask[:, :, None, None], axis=1)


def spread_block(values, block_mask):
    rows_local, block_size, token_count = values.shape
    sub_count = block_mask.shape[1]
    spread = values[:, None, :, :] * block_mask[:, :, None, None]
    return spread.reshape(rows_local, sub_count * block_size, token_count)


def pick_rows(received, row_mask):
    mesh_row_count, rows_local, token_count = received.shape
    sub_count = row_mask.shape[0]
    split = received.reshape(mesh_row_count // sub_count, sub_count, rows_local, token_count)
    return jnp.sum(split * row_mask[None, :, :, None], axis=1)


def paired_product(segment, weight, block_size):
    token_count, width = segment.shape
    grid_local = weight.shape[1] // (2 * block_size)
    weight_rows = weight
    weight_rows = weight_rows.reshape(width // 2, grid_local, 2, block_size)
    pairs = segment.reshape(token_count, width // 2, 2)
    partial_value = jnp.einsum(
        "trs,rgsc->tgc", pairs, weight_rows, preferred_element_type=jnp.float32
    )
    return partial_value.reshape(token_count, grid_local * block_size)


def base_product(x_local, weight, block_size):
    return paired_product(lax.all_gather(x_local, "tensor", axis=1, tiled=True), weight, block_size)


def rows_to_block_side(values, masks_pair):
    return pick_block(rows_direct(spread_rows(values, masks_pair[1])), masks_pair[0])


def block_to_row_side(values, masks_pair):
    return pick_rows(blocks_direct(spread_block(values, masks_pair[0])), masks_pair[1])


def one_step(x_local, target, base_out, right_factor, left_factor, masks_pair, step_size):
    token_count = x_local.shape[0]
    rows_local = right_factor.shape[0]
    block_size = right_factor.shape[1]
    sub_count = left_factor.shape[1] // block_size
    upper_right_half = right_factor.astype(jnp.bfloat16)
    left_half = left_factor.astype(jnp.bfloat16)
    input_mesh_grid = x_local.reshape(token_count, rows_local, block_size)
    base_rows = base_out.reshape(token_count, rows_local, block_size).transpose(2, 1, 0)
    target_rows = (
        target.reshape(token_count, rows_local, block_size).transpose(2, 1, 0).astype(jnp.float32)
    )
    offset = (base_rows - target_rows).astype(jnp.bfloat16)
    hidden = jnp.einsum(
        "ves,esl->lev", input_mesh_grid, upper_right_half, preferred_element_type=jnp.float32
    ).astype(jnp.bfloat16)
    gathered = toward_blocks(jnp.repeat(hidden, sub_count, axis=0))
    mixed_out = jnp.einsum(
        "sit,sik->skt", gathered, left_half, preferred_element_type=jnp.float32
    ).astype(jnp.bfloat16)
    output_rows = None
    mixed_rows = block_to_row_side(mixed_out, masks_pair)
    output_rows = base_rows + mixed_rows.astype(jnp.float32)
    error_rows = (offset.astype(jnp.float32) + mixed_rows.astype(jnp.float32)).astype(jnp.bfloat16)
    error_blocks = rows_to_block_side(error_rows, masks_pair)
    left_grad = jnp.einsum(
        "sit,skt->sik", gathered, error_blocks, preferred_element_type=jnp.float32
    )
    back_terms = jnp.einsum(
        "skt,sik->sit", error_blocks, left_half, preferred_element_type=jnp.float32
    ).astype(jnp.bfloat16)
    returned = toward_rows(back_terms)
    hidden_gradient = jnp.sum(
        returned.reshape(block_size, sub_count, rows_local, token_count).astype(jnp.float32), axis=1
    )
    right_grad = jnp.einsum(
        "wfm,sfw->fms",
        input_mesh_grid.astype(jnp.float32),
        hidden_gradient,
        precision=exact_precision,
    )
    right_grad, left_grad = lax.psum((right_grad, left_grad), "dp")
    return (output_rows, right_factor - step_size * right_grad, left_factor - step_size * left_grad)


def shards(
    x_first, target_first, x_second, target_second, frozen_weight_pairs, right_factor, left_factor
):
    rows_local = right_factor.shape[0]
    block_size = right_factor.shape[1]
    token_count = x_first.shape[0]
    masks_pair = make_masks(rows_local, left_factor.shape[1], block_size)
    step_size = 1.0 / (token_count * lax.axis_size("dp"))
    base_first = base_product(x_first, frozen_weight_pairs, block_size)
    unused, right_now, left_now = one_step(
        x_first, target_first, base_first, right_factor, left_factor, masks_pair, step_size
    )
    base_second = base_product(x_second, frozen_weight_pairs, block_size)
    output_rows, right_now, left_now = one_step(
        x_second, target_second, base_second, right_now, left_now, masks_pair, step_size
    )
    result = (
        output_rows.transpose(2, 1, 0)
        .reshape(token_count, rows_local * block_size)
        .astype(jnp.bfloat16)
    )
    return (result, right_now, left_now)


Z_COUNT, DEVICES, ROWS, COLS = 4, 16, 8, 4
PIECES = ((0, 0, 384), (1, 0, 256), (1, 256, 128))
PARTS = 2
RIGHT_IN, RIGHT_BACK, OFFSET, MIXED = 0, 1, 2, 2 + len(PIECES)
KINDS = 2 + 2 * len(PIECES)


def adapter_kernel(
    step_size, x1, t1, x2, t2, weight, right_in, left_in, out, left_out, right_out,
    w, wd, xg, acc, base, rgrad, rhalf, lhalf, lturn, hid, hgrad, mixed, right_send, right_recv,
    back_send, back_recv, off_send, off_recv, mix_send, mix_recv,
    w_sem, ag_send, ag_recv, a2a_send, a2a_recv,
):
    tokens, width = x1.shape
    half = width // 2
    me = lax.axis_index("tensor")
    z, x, core = me // 4, lax.rem(me // 2, 2), lax.rem(me, 2)
    x_peer = z * 4 + (1 - x) * 2 + core
    core_peer = z * 4 + x * 2 + (1 - core)

    w_copy = pltpu.make_async_copy(weight, w, w_sem)
    w_copy.start()

    barrier = pltpu.get_barrier_semaphore()

    @pl.loop(1, DEVICES)
    def _(n):
        pl.semaphore_signal(
            barrier, inc=1, device_id={"tensor": lax.rem(me + n, DEVICES)}, device_id_type=MESH
        )

    row_id = lax.broadcasted_iota(jnp.int32, (width, width), 0)
    col_id = lax.broadcasted_iota(jnp.int32, (width, width), 1)
    split = jnp.where(row_id == 2 * lax.rem(col_id, half) + col_id // half, 1.0, 0.0).astype(BF)
    xg[0, me] = jnp.dot(x1[...], split, preferred_element_type=F32).astype(BF)

    pl.semaphore_wait(barrier, DEVICES - 1)

    def exchange(kind, source, target, peer, cut):
        return pltpu.make_async_remote_copy(
            src_ref=source.at[peer, :, cut],
            dst_ref=target.at[me, :, cut],
            send_sem=a2a_send.at[kind, peer],
            recv_sem=a2a_recv.at[kind, me],
            device_id={"tensor": peer},
            device_id_type=MESH,
        )

    def landed(kind, target, peer, cut):
        return pltpu.make_async_remote_copy(
            src_ref=target.at[peer, :, cut],
            dst_ref=target.at[peer, :, cut],
            send_sem=a2a_send.at[kind, peer],
            recv_sem=a2a_recv.at[kind, peer],
            device_id={"tensor": peer},
            device_id_type=MESH,
        )

    def send_all(kind, source, target, cut):
        @pl.loop(1, DEVICES)
        def _(n):
            exchange(kind, source, target, lax.rem(me + n, DEVICES), cut).start()

        target[me, :, cut] = source[me, :, cut]

    def wait_all(kind, target, cut):
        @pl.loop(1, DEVICES)
        def _(n):
            landed(kind, target, lax.rem(me + n, DEVICES), cut).wait_recv()

    def sent_all(kind, source, target, cut):
        @pl.loop(1, DEVICES)
        def _(n):
            exchange(kind, source, target, lax.rem(me + n, DEVICES), cut).wait_send()

    def span(piece):
        return slice(PIECES[piece][1], PIECES[piece][1] + PIECES[piece][2])

    def hop(piece, part, chunk, direction, peer):
        b, first, count = PIECES[piece]
        rows = slice(first + part * (count // PARTS), first + (part + 1) * (count // PARTS))
        return pltpu.make_async_remote_copy(
            src_ref=xg.at[b, chunk, rows],
            dst_ref=xg.at[b, chunk, rows],
            send_sem=ag_send.at[piece * PARTS + part, chunk, direction],
            recv_sem=ag_recv.at[piece * PARTS + part, chunk],
            device_id={"tensor": peer},
            device_id_type=MESH,
        )

    def z_order(k):
        high = z // 2
        mirrored = z * (1 - high) + (3 - z) * high
        order = k + (1 - k // 2) * mirrored * (1 - 2 * k)
        return order * (1 - high) + (3 - order) * high

    def along_z(piece, part, source_z, act):
        chunk = source_z * 4 + x * 2 + core

        @pl.when((source_z <= z) & (z < Z_COUNT - 1))
        def _():
            act(hop(piece, part, chunk, 0, me + 4))

        @pl.when((source_z >= z) & (z > 0))
        def _():
            act(hop(piece, part, chunk, 1, me - 4))

    def across(piece, part, source_z, act):
        chunk = source_z * 4 + x * 2 + core
        act(hop(piece, part, chunk, 2, x_peer))
        act(hop(piece, part, chunk, 3, core_peer))

    def start(copy):
        copy.start()

    def apply_base(piece, chunk):
        b, cut = PIECES[piece][0], span(piece)
        acc[cut, :] += jnp.dot(xg[b, chunk, cut, :], wd[chunk], preferred_element_type=F32)

    def apply_hidden(piece, chunk):
        b, cut = PIECES[piece][0], span(piece)
        value = lax.dot_general(
            rhalf[chunk], xg[b, chunk, cut, :], LANES, preferred_element_type=F32
        )
        for d in range(COLS):
            hid[d, pl.ds(pl.multiple_of(chunk * ROWS, ROWS), ROWS), cut] = value[
                d * ROWS : (d + 1) * ROWS
            ]

    def landed_all(piece, chunk):
        for part in range(PARTS):
            hop(piece, part, chunk, 3, core_peer).wait_recv()

    def use(piece, chunk, with_hidden):
        apply_base(piece, chunk)
        if with_hidden:
            apply_hidden(piece, chunk)

    def use_own(piece, k, with_hidden):
        def one(m, carry):
            chunk = z_order(k) * 4 + x * 2 + core + m * (1 - 2 * core)

            @pl.when(m > 0)
            def _():
                landed_all(piece, chunk)

            use(piece, chunk, with_hidden)
            return carry

        lax.fori_loop(0, 2, one, 0)

    def use_other(piece, k, with_hidden):
        def one(m, carry):
            chunk = z_order(k) * 4 + (1 - x) * 2 + core + m * (1 - 2 * core)

            @pl.when(m > 0)
            def _():
                landed_all(piece, chunk)

            use(piece, chunk, with_hidden)
            return carry

        lax.fori_loop(0, 2, one, 0)

    def gather(piece, first, last, with_hidden):
        ahead = piece + 1 if piece + 1 < len(PIECES) else None

        def from_z(part, k):
            @pl.when(k < 3)
            def _():
                next_z = z_order(k + 1)
                hop(piece, part, next_z * 4 + x * 2 + core, 3, core_peer).wait_recv()
                along_z(piece, part, next_z, start)
                across(piece, part, next_z, start)

        def from_x(part, k):
            copy = hop(piece, part, z_order(k) * 4 + (1 - x) * 2 + core, 3, core_peer)
            copy.wait_recv()
            copy.start()

        def body(k, carry):
            from_z(0, k)
            if ahead is not None:

                @pl.when(k == 3)
                def _():
                    for part in range(PARTS):
                        across(ahead, part, z, start)

            from_x(0, k)

            @pl.when(k > 0)
            def _():
                use_other(piece, k - 1, with_hidden)

            from_z(1, k)
            if ahead is not None:

                @pl.when(k == 2)
                def _():
                    for part in range(PARTS):
                        along_z(ahead, part, z, start)

            from_x(1, k)
            use_own(piece, k, with_hidden)
            return carry

        lax.fori_loop(first, last, body, 0)
        if last == 4:
            use_other(piece, 3, with_hidden)

    def sent_gather(piece):
        for part in range(PARTS):

            @pl.loop(0, Z_COUNT)
            def _(source_z):
                along_z(piece, part, source_z, lambda copy: copy.wait_send())
                across(piece, part, source_z, lambda copy: copy.wait_send())
                hop(
                    piece, part, source_z * 4 + (1 - x) * 2 + core, 3, core_peer
                ).wait_send()

    def clear(piece):
        acc[span(piece), :] = jnp.zeros((PIECES[piece][2], width), F32)

    def finish_base(piece, target):
        b, cut, count = PIECES[piece][0], span(piece), PIECES[piece][2]
        value = acc[cut, :]
        if b == 1:
            base[cut, :] = value
        offset = (value - target[cut, :].astype(F32)).astype(BF)
        turned = lax.dot_general(turn, offset, LANES, preferred_element_type=F32)
        off_send[b, :, :, cut] = turned.astype(BF).reshape(DEVICES, COLS * ROWS, count)
        send_all(OFFSET + piece, off_send.at[b], off_recv.at[b], cut)

    def take_left(ref):
        for d in range(COLS):
            pair = jnp.concatenate([ref[2 * d], ref[2 * d + 1]], axis=0)
            lturn[d] = pair.astype(BF)
            lhalf[d] = pair.T.astype(BF)

    def mix(piece):
        cut = span(piece)
        for d in range(COLS):
            mixed[d, :, cut] = (
                jnp.dot(lturn[d], hid[d, :, cut].astype(BF), preferred_element_type=F32)
                .astype(BF)
                .astype(F32)
            )

    def send_mixed(piece):
        cut, count = span(piece), PIECES[piece][2]
        stacked = jnp.stack(
            [mixed[d, :, cut].reshape(DEVICES, ROWS, count) for d in range(COLS)], axis=1
        )
        mix_send[:, :, cut] = stacked.reshape(DEVICES, COLS * ROWS, count).astype(BF)
        send_all(MIXED + piece, mix_send, mix_recv, cut)

    block_row = lax.broadcasted_iota(jnp.int32, (COLS * ROWS, width), 0)
    block_col = lax.broadcasted_iota(jnp.int32, (COLS * ROWS, width), 1)
    on_block = lax.rem(block_row, ROWS) == lax.rem(block_col, half) // (half // ROWS)

    def backward(piece):
        b, cut, count = PIECES[piece][0], span(piece), PIECES[piece][2]
        wait_all(OFFSET + piece, off_recv.at[b], cut)
        received = off_recv[b, :, :, cut].astype(F32).reshape(DEVICES, COLS, ROWS, count)
        for d in range(COLS):
            offset = received[:, d].reshape(DEVICES * ROWS, count)
            error = (offset + mixed[d, :, cut]).astype(BF)
            hgrad[d, :, cut] = jnp.dot(lhalf[d], error, preferred_element_type=F32)
            grad = step_size * lax.dot_general(
                error, hid[d, :, cut].astype(BF), LANES, preferred_element_type=F32
            )
            left_out[2 * d] = left_out[2 * d] - grad[:64]
            left_out[2 * d + 1] = left_out[2 * d + 1] - grad[64:]

        @pl.loop(0, DEVICES)
        def _(chunk):
            rows = pl.ds(pl.multiple_of(chunk * ROWS, ROWS), ROWS)
            left = jnp.concatenate([hgrad[d, rows, cut] for d in range(COLS)], axis=0).astype(BF)
            grad = jnp.dot(left, xg[b, chunk, cut, :], preferred_element_type=F32)
            rgrad[chunk] = rgrad[chunk] + jnp.where(on_block, grad, 0.0)

    small_lane = lax.broadcasted_iota(jnp.int32, (COLS * ROWS, 128), 1)

    def take_right():
        @pl.loop(0, DEVICES)
        def _(chunk):
            value = right_recv[chunk].astype(F32)
            turned = pltpu.roll(value, 64, 1)
            even = jnp.where(small_lane < 64, value, turned)
            odd = jnp.where(small_lane < 64, turned, value)
            full = jnp.where(on_block, jnp.concatenate([even, even, odd, odd], axis=1), 0.0)
            rhalf[chunk] = (full - step_size * rgrad[chunk]).astype(BF)

    def give_output(piece):
        cut, count = span(piece), PIECES[piece][2]
        wait_all(MIXED + piece, mix_recv, cut)
        rows_in = mix_recv[:, :, cut].reshape(DEVICES * COLS * ROWS, count).astype(F32)
        mixed_rows = jnp.dot(rows_in.T.astype(BF), turn, preferred_element_type=F32)
        out[cut, :] = (base[cut, :] + mixed_rows).astype(BF)

    for part in range(PARTS):
        along_z(0, part, z, start)
        across(0, part, z, start)

    block_id = lax.broadcasted_iota(jnp.int32, (64, 128), 0)
    lane_id = lax.broadcasted_iota(jnp.int32, (64, 128), 1)
    own_lane = block_id == 2 * lax.rem(lane_id, 32) + lane_id // 64
    pairs = jnp.where(own_lane, 1.0, 0.0).astype(BF)
    one_pair = jnp.where(own_lane & (lax.rem(lane_id, 64) < 32), 1.0, 0.0).astype(BF)
    spread = [
        jnp.dot(right_in[i].T.astype(BF), pairs, preferred_element_type=F32) for i in range(ROWS)
    ]
    right_send[...] = (
        jnp.stack(spread, axis=1).reshape(DEVICES, COLS * ROWS, 128).astype(BF)
    )
    lanes = slice(0, 128)
    send_all(RIGHT_IN, right_send, right_recv, lanes)

    xg[1, me] = jnp.dot(x2[...], split, preferred_element_type=F32).astype(BF)
    turn = jnp.where(
        col_id == lax.rem(row_id, ROWS) * (width // ROWS) + row_id // ROWS, 1.0, 0.0
    ).astype(BF)
    rgrad[...] = jnp.zeros_like(rgrad)
    left_out[...] = left_in[...]
    take_left(left_in)
    clear(0)
    w_copy.wait()
    low = lax.broadcasted_iota(jnp.int32, (half, 128), 1) < 64

    @pl.loop(0, DEVICES)
    def _(chunk):
        rows = pl.ds(pl.multiple_of(chunk * half, half), half)
        for n in range(width // 128):
            first = w[rows, 256 * n : 256 * n + 128]
            second = w[rows, 256 * n + 128 : 256 * n + 256]
            lanes_n = slice(128 * n, 128 * n + 128)
            wd[chunk, :half, lanes_n] = jnp.concatenate([first[:, :64], second[:, :64]], axis=1)
            wd[chunk, half:, lanes_n] = jnp.concatenate([first[:, 64:], second[:, 64:]], axis=1)


    def early(piece, steps):
        def one(m, carry):
            apply_hidden(piece, z_order(m // 4) * 4 + lax.rem(x * 2 + lax.rem(m, 4), 4))
            return carry

        lax.fori_loop(0, 4 * steps - 2, one, 0)

    gather(0, 0, 2, False)
    wait_all(RIGHT_IN, right_recv, lanes)
    take_right()
    early(0, 2)
    gather(0, 2, 4, True)
    finish_base(0, t1)
    clear(1)
    clear(2)
    mix(0)
    gather(1, 0, 3, False)
    backward(0)
    take_left(left_out)
    take_right()
    early(1, 3)
    gather(1, 3, 4, True)
    finish_base(1, t2)
    mix(1)
    send_mixed(1)
    gather(2, 0, 4, True)
    finish_base(2, t2)
    mix(2)
    send_mixed(2)
    backward(1)
    give_output(1)
    backward(2)

    @pl.loop(0, DEVICES)
    def _(chunk):
        value = rgrad[chunk]
        folded = []
        for s in range(2):
            part = value[:, s * half : s * half + 128] + value[:, s * half + 128 : (s + 1) * half]
            part = part + pltpu.roll(part, 64, 1)
            folded.append(part + pltpu.roll(part, 32, 1))
        back_send[chunk] = jnp.where(small_lane < 64, folded[0], folded[1]).astype(BF)

    send_all(RIGHT_BACK, back_send, back_recv, lanes)
    give_output(2)
    for piece in range(len(PIECES)):
        sent_gather(piece)
        b = PIECES[piece][0]
        sent_all(OFFSET + piece, off_send.at[b], off_recv.at[b], span(piece))
        if b == 1:
            sent_all(MIXED + piece, mix_send, mix_recv, span(piece))
    sent_all(RIGHT_IN, right_send, right_recv, lanes)
    wait_all(RIGHT_BACK, back_recv, lanes)
    returned = back_recv[...].astype(F32).reshape(DEVICES * COLS, ROWS, 128)
    for i in range(ROWS):
        grad = lax.dot_general(
            one_pair, returned[:, i, :].astype(BF), LANES, preferred_element_type=F32
        )
        right_out[i] = right_in[i] - step_size * grad

    sent_all(RIGHT_BACK, back_send, back_recv, lanes)


def hand_over(out, left, right, out_to, left_to, right_to):
    out_to[...] = out[...]
    left_to[...] = left[...]
    right_to[...] = right[...]


def fused_shards(
    x_first, target_first, x_second, target_second, frozen_weight_pairs, right_factor, left_factor
):
    tokens, width = x_first.shape
    step_size = 1.0 / tokens
    left_turned = jnp.swapaxes(left_factor, 1, 2)
    vmem = pl.BlockSpec(memory_space=pltpu.VMEM)
    slab = (DEVICES, COLS * ROWS, tokens)
    small = pltpu.VMEM((DEVICES, COLS * ROWS, 128), BF)
    cols = pltpu.VMEM((COLS, DEVICES * ROWS, tokens), F32)
    square = pltpu.VMEM((COLS, 128, 128), BF)
    out, left_now, right_now = pl.pallas_call(
        functools.partial(adapter_kernel, step_size),
        out_shape=(
            jax.ShapeDtypeStruct((tokens, width), BF),
            jax.ShapeDtypeStruct(left_turned.shape, F32),
            jax.ShapeDtypeStruct(right_factor.shape, F32),
        ),
        in_specs=[vmem] * 4 + [pl.BlockSpec(memory_space=pl.ANY)] + [vmem] * 2,
        out_specs=(vmem, vmem, vmem),
        scratch_shapes=[
            pltpu.VMEM(frozen_weight_pairs.shape, BF),
            pltpu.VMEM((DEVICES, width, width), BF),
            pltpu.VMEM((2, DEVICES, tokens, width), BF),
            pltpu.VMEM((tokens, width), F32),
            pltpu.VMEM((tokens, width), F32),
            pltpu.VMEM((DEVICES, COLS * ROWS, width), F32),
            pltpu.VMEM((DEVICES, COLS * ROWS, width), BF),
            square,
            square,
            cols,
            cols,
            cols,
            small,
            small,
            small,
            small,
            pltpu.VMEM((2,) + slab, BF),
            pltpu.VMEM((2,) + slab, BF),
            pltpu.VMEM(slab, BF),
            pltpu.VMEM(slab, BF),
            pltpu.SemaphoreType.DMA,
            pltpu.SemaphoreType.DMA((len(PIECES) * PARTS, DEVICES, 4)),
            pltpu.SemaphoreType.DMA((len(PIECES) * PARTS, DEVICES)),
            pltpu.SemaphoreType.DMA((KINDS, DEVICES)),
            pltpu.SemaphoreType.DMA((KINDS, DEVICES)),
        ],
        compiler_params=pltpu.CompilerParams(
            collective_id=0, has_side_effects=True, vmem_limit_bytes=60 * 1024 * 1024
        ),
        name="adapter",
    )(
        x_first, target_first, x_second, target_second, frozen_weight_pairs, right_factor, left_turned
    )
    results = (out, left_now, right_now)
    out, left_now, right_now = pl.pallas_call(
        hand_over,
        out_shape=tuple(jax.ShapeDtypeStruct(a.shape, a.dtype) for a in results),
        in_specs=[vmem] * 3,
        out_specs=(vmem,) * 3,
        name="hand_over",
    )(*results)
    return (out, right_now, jnp.swapaxes(left_now, 1, 2))


def solution(mesh):
    fused = mesh.shape["tensor"] == DEVICES and mesh.shape["dp"] == 1
    body = fused_shards if fused else shards
    return jax.shard_map(
        body,
        mesh=mesh,
        in_specs=(
            P(("groups", "dp"), "tensor"),
            P(("groups", "dp"), "tensor"),
            P(("groups", "dp"), "tensor"),
            P(("groups", "dp"), "tensor"),
            P(None, "tensor"),
            P(("groups", "tensor"), None, None),
            P(("groups", "tensor"), None, None),
        ),
        out_specs=(
            P(("groups", "dp"), "tensor"),
            P(("groups", "tensor"), None, None),
            P(("groups", "tensor"), None, None),
        ),
        check_vma=False,
    )
```

```python
import functools

import jax
import jax.numpy as jnp
from jax import lax
from jax.experimental import pallas as pl
from jax.experimental.pallas import tpu as pltpu
from jax.sharding import PartitionSpec as P

MESH = pl.DeviceIdType.MESH
BF = jnp.bfloat16
F32 = jnp.float32
LANES = (((1,), (1,)), ((), ()))

exact_precision = lax.Precision.HIGHEST


def toward_blocks(buffer_rows):
    return lax.all_to_all(buffer_rows, "tensor", split_axis=0, concat_axis=1, tiled=True)


def toward_rows(buffer_blocks):
    return lax.all_to_all(buffer_blocks, "tensor", split_axis=1, concat_axis=0, tiled=True)


def rows_direct(buffer_rows):
    return lax.all_to_all(buffer_rows, "tensor", split_axis=0, concat_axis=1, tiled=True)


def blocks_direct(buffer_blocks):
    return lax.all_to_all(buffer_blocks, "tensor", split_axis=1, concat_axis=0, tiled=True)


def make_masks(rows_local, mesh_row_count, block_size):
    sub_count = mesh_row_count // block_size
    own_index = lax.axis_index("tensor") * rows_local + jnp.arange(rows_local, dtype=jnp.int32)
    positions = jnp.arange(sub_count, dtype=jnp.int32)
    block_mask = (positions[None, :] == (own_index % sub_count)[:, None]).astype(jnp.bfloat16)
    row_mask = (positions[:, None] == (own_index // block_size)[None, :]).astype(jnp.bfloat16)
    return (block_mask, row_mask)


def spread_rows(values, row_mask):
    block_size, rows_local, token_count = values.shape
    sub_count = row_mask.shape[0]
    spread = values[:, None, :, :] * row_mask[None, :, :, None]
    return spread.reshape(block_size * sub_count, rows_local, token_count)


def pick_block(received, block_mask):
    rows_local, mesh_row_count, token_count = received.shape
    sub_count = block_mask.shape[1]
    split = received.reshape(rows_local, sub_count, mesh_row_count // sub_count, token_count)
    return jnp.sum(split * block_mask[:, :, None, None], axis=1)


def spread_block(values, block_mask):
    rows_local, block_size, token_count = values.shape
    sub_count = block_mask.shape[1]
    spread = values[:, None, :, :] * block_mask[:, :, None, None]
    return spread.reshape(rows_local, sub_count * block_size, token_count)


def pick_rows(received, row_mask):
    mesh_row_count, rows_local, token_count = received.shape
    sub_count = row_mask.shape[0]
    split = received.reshape(mesh_row_count // sub_count, sub_count, rows_local, token_count)
    return jnp.sum(split * row_mask[None, :, :, None], axis=1)


def paired_product(segment, weight, block_size):
    token_count, width = segment.shape
    grid_local = weight.shape[1] // (2 * block_size)
    weight_rows = weight
    weight_rows = weight_rows.reshape(width // 2, grid_local, 2, block_size)
    pairs = segment.reshape(token_count, width // 2, 2)
    partial_value = jnp.einsum(
        "trs,rgsc->tgc", pairs, weight_rows, preferred_element_type=jnp.float32
    )
    return partial_value.reshape(token_count, grid_local * block_size)


def base_product(x_local, weight, block_size):
    return paired_product(lax.all_gather(x_local, "tensor", axis=1, tiled=True), weight, block_size)


def rows_to_block_side(values, masks_pair):
    return pick_block(rows_direct(spread_rows(values, masks_pair[1])), masks_pair[0])


def block_to_row_side(values, masks_pair):
    return pick_rows(blocks_direct(spread_block(values, masks_pair[0])), masks_pair[1])


def one_step(x_local, target, base_out, right_factor, left_factor, masks_pair, step_size):
    token_count = x_local.shape[0]
    rows_local = right_factor.shape[0]
    block_size = right_factor.shape[1]
    sub_count = left_factor.shape[1] // block_size
    upper_right_half = right_factor.astype(jnp.bfloat16)
    left_half = left_factor.astype(jnp.bfloat16)
    input_mesh_grid = x_local.reshape(token_count, rows_local, block_size)
    base_rows = base_out.reshape(token_count, rows_local, block_size).transpose(2, 1, 0)
    target_rows = (
        target.reshape(token_count, rows_local, block_size).transpose(2, 1, 0).astype(jnp.float32)
    )
    offset = (base_rows - target_rows).astype(jnp.bfloat16)
    hidden = jnp.einsum(
        "ves,esl->lev", input_mesh_grid, upper_right_half, preferred_element_type=jnp.float32
    ).astype(jnp.bfloat16)
    gathered = toward_blocks(jnp.repeat(hidden, sub_count, axis=0))
    mixed_out = jnp.einsum(
        "sit,sik->skt", gathered, left_half, preferred_element_type=jnp.float32
    ).astype(jnp.bfloat16)
    output_rows = None
    mixed_rows = block_to_row_side(mixed_out, masks_pair)
    output_rows = base_rows + mixed_rows.astype(jnp.float32)
    error_rows = (offset.astype(jnp.float32) + mixed_rows.astype(jnp.float32)).astype(jnp.bfloat16)
    error_blocks = rows_to_block_side(error_rows, masks_pair)
    left_grad = jnp.einsum(
        "sit,skt->sik", gathered, error_blocks, preferred_element_type=jnp.float32
    )
    back_terms = jnp.einsum(
        "skt,sik->sit", error_blocks, left_half, preferred_element_type=jnp.float32
    ).astype(jnp.bfloat16)
    returned = toward_rows(back_terms)
    hidden_gradient = jnp.sum(
        returned.reshape(block_size, sub_count, rows_local, token_count).astype(jnp.float32), axis=1
    )
    right_grad = jnp.einsum(
        "wfm,sfw->fms",
        input_mesh_grid.astype(jnp.float32),
        hidden_gradient,
        precision=exact_precision,
    )
    right_grad, left_grad = lax.psum((right_grad, left_grad), "dp")
    return (output_rows, right_factor - step_size * right_grad, left_factor - step_size * left_grad)


def shards(
    x_first, target_first, x_second, target_second, frozen_weight_pairs, right_factor, left_factor
):
    rows_local = right_factor.shape[0]
    block_size = right_factor.shape[1]
    token_count = x_first.shape[0]
    masks_pair = make_masks(rows_local, left_factor.shape[1], block_size)
    step_size = 1.0 / (token_count * lax.axis_size("dp"))
    base_first = base_product(x_first, frozen_weight_pairs, block_size)
    unused, right_now, left_now = one_step(
        x_first, target_first, base_first, right_factor, left_factor, masks_pair, step_size
    )
    base_second = base_product(x_second, frozen_weight_pairs, block_size)
    output_rows, right_now, left_now = one_step(
        x_second, target_second, base_second, right_now, left_now, masks_pair, step_size
    )
    result = (
        output_rows.transpose(2, 1, 0)
        .reshape(token_count, rows_local * block_size)
        .astype(jnp.bfloat16)
    )
    return (result, right_now, left_now)


Z_COUNT, DEVICES, ROWS, COLS = 4, 16, 8, 4
PIECES = ((0, 0, 384), (1, 0, 256), (1, 256, 128))
PARTS = 2
RIGHT_IN, RIGHT_BACK, OFFSET, MIXED = 0, 1, 2, 2 + len(PIECES)
KINDS = 2 + 2 * len(PIECES)


def adapter_kernel(
    step_size, x1, t1, x2, t2, weight, right_in, left_in, out, left_out, right_out,
    w, wd, xg, acc, base, rgrad, rhalf, lhalf, lturn, hid, hgrad, mixed, right_send, right_recv,
    back_send, back_recv, off_send, off_recv, mix_send, mix_recv,
    w_sem, ag_send, ag_recv, a2a_send, a2a_recv,
):
    tokens, width = x1.shape
    half = width // 2
    me = lax.axis_index("tensor")
    z, x, core = me // 4, lax.rem(me // 2, 2), lax.rem(me, 2)
    x_peer = z * 4 + (1 - x) * 2 + core
    core_peer = z * 4 + x * 2 + (1 - core)

    w_copy = pltpu.make_async_copy(weight, w, w_sem)
    w_copy.start()

    barrier = pltpu.get_barrier_semaphore()

    @pl.loop(1, DEVICES)
    def _(n):
        pl.semaphore_signal(
            barrier, inc=1, device_id={"tensor": lax.rem(me + n, DEVICES)}, device_id_type=MESH
        )

    row_id = lax.broadcasted_iota(jnp.int32, (width, width), 0)
    col_id = lax.broadcasted_iota(jnp.int32, (width, width), 1)
    split = jnp.where(row_id == ((col_id & (half - 1)) << 1) + (col_id >> (half.bit_length() - 1)), 1.0, 0.0).astype(BF)
    xg[0, me] = jnp.dot(x1[...], split, preferred_element_type=F32).astype(BF)

    pl.semaphore_wait(barrier, DEVICES - 1)

    def exchange(kind, source, target, peer, cut):
        return pltpu.make_async_remote_copy(
            src_ref=source.at[peer, :, cut],
            dst_ref=target.at[me, :, cut],
            send_sem=a2a_send.at[kind, peer],
            recv_sem=a2a_recv.at[kind, me],
            device_id={"tensor": peer},
            device_id_type=MESH,
        )

    def landed(kind, target, peer, cut):
        return pltpu.make_async_remote_copy(
            src_ref=target.at[peer, :, cut],
            dst_ref=target.at[peer, :, cut],
            send_sem=a2a_send.at[kind, peer],
            recv_sem=a2a_recv.at[kind, peer],
            device_id={"tensor": peer},
            device_id_type=MESH,
        )

    def send_all(kind, source, target, cut):
        @pl.loop(1, DEVICES)
        def _(n):
            exchange(kind, source, target, lax.rem(me + n, DEVICES), cut).start()

        target[me, :, cut] = source[me, :, cut]

    def wait_all(kind, target, cut):
        @pl.loop(1, DEVICES)
        def _(n):
            landed(kind, target, lax.rem(me + n, DEVICES), cut).wait_recv()

    def sent_all(kind, source, target, cut):
        @pl.loop(1, DEVICES)
        def _(n):
            exchange(kind, source, target, lax.rem(me + n, DEVICES), cut).wait_send()

    def span(piece):
        return slice(PIECES[piece][1], PIECES[piece][1] + PIECES[piece][2])

    def hop(piece, part, chunk, direction, peer):
        b, first, count = PIECES[piece]
        rows = slice(first + part * (count // PARTS), first + (part + 1) * (count // PARTS))
        return pltpu.make_async_remote_copy(
            src_ref=xg.at[b, chunk, rows],
            dst_ref=xg.at[b, chunk, rows],
            send_sem=ag_send.at[piece * PARTS + part, chunk, direction],
            recv_sem=ag_recv.at[piece * PARTS + part, chunk],
            device_id={"tensor": peer},
            device_id_type=MESH,
        )

    def z_order(k):
        high = z // 2
        mirrored = z * (1 - high) + (3 - z) * high
        order = k + (1 - k // 2) * mirrored * (1 - 2 * k)
        return order * (1 - high) + (3 - order) * high

    def along_z(piece, part, source_z, act):
        chunk = source_z * 4 + x * 2 + core

        @pl.when((source_z <= z) & (z < Z_COUNT - 1))
        def _():
            act(hop(piece, part, chunk, 0, me + 4))

        @pl.when((source_z >= z) & (z > 0))
        def _():
            act(hop(piece, part, chunk, 1, me - 4))

    def across(piece, part, source_z, act):
        chunk = source_z * 4 + x * 2 + core
        act(hop(piece, part, chunk, 2, x_peer))
        act(hop(piece, part, chunk, 3, core_peer))

    def start(copy):
        copy.start()

    def apply_base(piece, chunk):
        b, cut = PIECES[piece][0], span(piece)
        acc[cut, :] += jnp.dot(xg[b, chunk, cut, :], wd[chunk], preferred_element_type=F32)

    def apply_hidden(piece, chunk):
        b, cut = PIECES[piece][0], span(piece)
        value = lax.dot_general(
            rhalf[chunk], xg[b, chunk, cut, :], LANES, preferred_element_type=F32
        )
        for d in range(COLS):
            hid[d, pl.ds(pl.multiple_of(chunk * ROWS, ROWS), ROWS), cut] = value[
                d * ROWS : (d + 1) * ROWS
            ]

    def landed_all(piece, chunk):
        for part in range(PARTS):
            hop(piece, part, chunk, 3, core_peer).wait_recv()

    def use(piece, chunk, with_hidden):
        apply_base(piece, chunk)
        if with_hidden:
            apply_hidden(piece, chunk)

    def use_own(piece, k, with_hidden):
        def one(m, carry):
            chunk = z_order(k) * 4 + x * 2 + core + m * (1 - 2 * core)

            @pl.when(m > 0)
            def _():
                landed_all(piece, chunk)

            use(piece, chunk, with_hidden)
            return carry

        lax.fori_loop(0, 2, one, 0)

    def use_other(piece, k, with_hidden):
        def one(m, carry):
            chunk = z_order(k) * 4 + (1 - x) * 2 + core + m * (1 - 2 * core)

            @pl.when(m > 0)
            def _():
                landed_all(piece, chunk)

            use(piece, chunk, with_hidden)
            return carry

        lax.fori_loop(0, 2, one, 0)

    def gather(piece, first, last, with_hidden):
        ahead = piece + 1 if piece + 1 < len(PIECES) else None

        def from_z(part, k):
            @pl.when(k < 3)
            def _():
                next_z = z_order(k + 1)
                hop(piece, part, next_z * 4 + x * 2 + core, 3, core_peer).wait_recv()
                along_z(piece, part, next_z, start)
                across(piece, part, next_z, start)

        def from_x(part, k):
            copy = hop(piece, part, z_order(k) * 4 + (1 - x) * 2 + core, 3, core_peer)
            copy.wait_recv()
            copy.start()

        def body(k, carry):
            from_z(0, k)
            if ahead is not None:

                @pl.when(k == 3)
                def _():
                    for part in range(PARTS):
                        across(ahead, part, z, start)

            from_x(0, k)

            @pl.when(k > 0)
            def _():
                use_other(piece, k - 1, with_hidden)

            from_z(1, k)
            if ahead is not None:

                @pl.when(k == 2)
                def _():
                    for part in range(PARTS):
                        along_z(ahead, part, z, start)

            from_x(1, k)
            use_own(piece, k, with_hidden)
            return carry

        lax.fori_loop(first, last, body, 0)
        if last == 4:
            use_other(piece, 3, with_hidden)

    def sent_gather(piece):
        for part in range(PARTS):

            @pl.loop(0, Z_COUNT)
            def _(source_z):
                along_z(piece, part, source_z, lambda copy: copy.wait_send())
                across(piece, part, source_z, lambda copy: copy.wait_send())
                hop(
                    piece, part, source_z * 4 + (1 - x) * 2 + core, 3, core_peer
                ).wait_send()

    def clear(piece):
        acc[span(piece), :] = jnp.zeros((PIECES[piece][2], width), F32)

    def finish_base(piece, target):
        b, cut, count = PIECES[piece][0], span(piece), PIECES[piece][2]
        value = acc[cut, :]
        if b == 1:
            base[cut, :] = value
        offset = (value - target[cut, :].astype(F32)).astype(BF)
        turned = lax.dot_general(turn, offset, LANES, preferred_element_type=F32)
        off_send[b, :, :, cut] = turned.astype(BF).reshape(DEVICES, COLS * ROWS, count)
        send_all(OFFSET + piece, off_send.at[b], off_recv.at[b], cut)

    def take_left(ref):
        for d in range(COLS):
            pair = jnp.concatenate([ref[2 * d], ref[2 * d + 1]], axis=0)
            lturn[d] = pair.astype(BF)
            lhalf[d] = pair.T.astype(BF)

    def mix(piece):
        cut = span(piece)
        for d in range(COLS):
            mixed[d, :, cut] = (
                jnp.dot(lturn[d], hid[d, :, cut].astype(BF), preferred_element_type=F32)
                .astype(BF)
                .astype(F32)
            )

    def send_mixed(piece):
        cut, count = span(piece), PIECES[piece][2]
        stacked = jnp.stack(
            [mixed[d, :, cut].reshape(DEVICES, ROWS, count) for d in range(COLS)], axis=1
        )
        mix_send[:, :, cut] = stacked.reshape(DEVICES, COLS * ROWS, count).astype(BF)
        send_all(MIXED + piece, mix_send, mix_recv, cut)

    block_row = lax.broadcasted_iota(jnp.int32, (COLS * ROWS, width), 0)
    block_col = lax.broadcasted_iota(jnp.int32, (COLS * ROWS, width), 1)
    on_block = lax.rem(block_row, ROWS) == lax.rem(block_col, half) // (half // ROWS)

    def backward(piece):
        b, cut, count = PIECES[piece][0], span(piece), PIECES[piece][2]
        wait_all(OFFSET + piece, off_recv.at[b], cut)
        received = off_recv[b, :, :, cut].astype(F32).reshape(DEVICES, COLS, ROWS, count)
        for d in range(COLS):
            offset = received[:, d].reshape(DEVICES * ROWS, count)
            error = (offset + mixed[d, :, cut]).astype(BF)
            hgrad[d, :, cut] = jnp.dot(lhalf[d], error, preferred_element_type=F32)
            grad = step_size * lax.dot_general(
                error, hid[d, :, cut].astype(BF), LANES, preferred_element_type=F32
            )
            left_out[2 * d] = left_out[2 * d] - grad[:64]
            left_out[2 * d + 1] = left_out[2 * d + 1] - grad[64:]

        @pl.loop(0, DEVICES)
        def _(chunk):
            rows = pl.ds(pl.multiple_of(chunk * ROWS, ROWS), ROWS)
            left = jnp.concatenate([hgrad[d, rows, cut] for d in range(COLS)], axis=0).astype(BF)
            grad = jnp.dot(left, xg[b, chunk, cut, :], preferred_element_type=F32)
            rgrad[chunk] = rgrad[chunk] + jnp.where(on_block, grad, 0.0)

    small_lane = lax.broadcasted_iota(jnp.int32, (COLS * ROWS, 128), 1)

    def take_right():
        @pl.loop(0, DEVICES)
        def _(chunk):
            value = right_recv[chunk].astype(F32)
            turned = pltpu.roll(value, 64, 1)
            even = jnp.where(small_lane < 64, value, turned)
            odd = jnp.where(small_lane < 64, turned, value)
            full = jnp.where(on_block, jnp.concatenate([even, even, odd, odd], axis=1), 0.0)
            rhalf[chunk] = (full - step_size * rgrad[chunk]).astype(BF)

    def give_output(piece):
        cut, count = span(piece), PIECES[piece][2]
        wait_all(MIXED + piece, mix_recv, cut)
        rows_in = mix_recv[:, :, cut].reshape(DEVICES * COLS * ROWS, count).astype(F32)
        mixed_rows = jnp.dot(rows_in.T.astype(BF), turn, preferred_element_type=F32)
        out[cut, :] = (base[cut, :] + mixed_rows).astype(BF)

    for part in range(PARTS):
        along_z(0, part, z, start)
        across(0, part, z, start)

    block_id = lax.broadcasted_iota(jnp.int32, (64, 128), 0)
    lane_id = lax.broadcasted_iota(jnp.int32, (64, 128), 1)
    own_lane = block_id == 2 * lax.rem(lane_id, 32) + lane_id // 64
    pairs = jnp.where(own_lane, 1.0, 0.0).astype(BF)
    one_pair = jnp.where(own_lane & (lax.rem(lane_id, 64) < 32), 1.0, 0.0).astype(BF)
    spread = [
        jnp.dot(right_in[i].T.astype(BF), pairs, preferred_element_type=F32) for i in range(ROWS)
    ]
    right_send[...] = (
        jnp.stack(spread, axis=1).reshape(DEVICES, COLS * ROWS, 128).astype(BF)
    )
    lanes = slice(0, 128)
    send_all(RIGHT_IN, right_send, right_recv, lanes)

    xg[1, me] = jnp.dot(x2[...], split, preferred_element_type=F32).astype(BF)
    turn = jnp.where(
        col_id == ((row_id & (ROWS - 1)) * (width // ROWS)) + (row_id >> (ROWS.bit_length() - 1)), 1.0, 0.0
    ).astype(BF)
    rgrad[...] = jnp.zeros_like(rgrad)
    left_out[...] = left_in[...]
    take_left(left_in)
    clear(0)
    w_copy.wait()
    low = lax.broadcasted_iota(jnp.int32, (half, 128), 1) < 64

    @pl.loop(0, DEVICES)
    def _(chunk):
        rows = pl.ds(pl.multiple_of(chunk * half, half), half)
        for n in range(width // 128):
            first = w[rows, 256 * n : 256 * n + 128]
            second = w[rows, 256 * n + 128 : 256 * n + 256]
            lanes_n = slice(128 * n, 128 * n + 128)
            wd[chunk, :half, lanes_n] = jnp.concatenate([first[:, :64], second[:, :64]], axis=1)
            wd[chunk, half:, lanes_n] = jnp.concatenate([first[:, 64:], second[:, 64:]], axis=1)


    def early(piece, steps):
        def one(m, carry):
            apply_hidden(piece, z_order(m // 4) * 4 + lax.rem(x * 2 + lax.rem(m, 4), 4))
            return carry

        lax.fori_loop(0, 4 * steps - 2, one, 0)

    gather(0, 0, 2, False)
    wait_all(RIGHT_IN, right_recv, lanes)
    take_right()
    early(0, 2)
    gather(0, 2, 4, True)
    finish_base(0, t1)
    clear(1)
    clear(2)
    mix(0)
    gather(1, 0, 3, False)
    backward(0)
    take_left(left_out)
    take_right()
    early(1, 3)
    gather(1, 3, 4, True)
    finish_base(1, t2)
    mix(1)
    gather(2, 0, 2, True)
    send_mixed(1)
    gather(2, 2, 4, True)
    finish_base(2, t2)
    mix(2)
    send_mixed(2)
    backward(1)
    give_output(1)
    backward(2)

    @pl.loop(0, DEVICES)
    def _(chunk):
        value = rgrad[chunk]
        folded = []
        for s in range(2):
            part = value[:, s * half : s * half + 128] + value[:, s * half + 128 : (s + 1) * half]
            part = part + pltpu.roll(part, 64, 1)
            folded.append(part + pltpu.roll(part, 32, 1))
        back_send[chunk] = jnp.where(small_lane < 64, folded[0], folded[1]).astype(BF)

    send_all(RIGHT_BACK, back_send, back_recv, lanes)
    give_output(2)
    for piece in range(len(PIECES)):
        sent_gather(piece)
        b = PIECES[piece][0]
        sent_all(OFFSET + piece, off_send.at[b], off_recv.at[b], span(piece))
        if b == 1:
            sent_all(MIXED + piece, mix_send, mix_recv, span(piece))
    sent_all(RIGHT_IN, right_send, right_recv, lanes)
    wait_all(RIGHT_BACK, back_recv, lanes)
    returned = back_recv[...].astype(F32).reshape(DEVICES * COLS, ROWS, 128)
    for i in range(ROWS):
        grad = lax.dot_general(
            one_pair, returned[:, i, :].astype(BF), LANES, preferred_element_type=F32
        )
        right_out[i] = right_in[i] - step_size * grad

    sent_all(RIGHT_BACK, back_send, back_recv, lanes)


def hand_over(out, left, right, out_to, left_to, right_to):
    out_to[...] = out[...]
    left_to[...] = left[...]
    right_to[...] = right[...]


def fused_shards(
    x_first, target_first, x_second, target_second, frozen_weight_pairs, right_factor, left_factor
):
    tokens, width = x_first.shape
    step_size = 1.0 / tokens
    left_turned = jnp.swapaxes(left_factor, 1, 2)
    vmem = pl.BlockSpec(memory_space=pltpu.VMEM)
    slab = (DEVICES, COLS * ROWS, tokens)
    small = pltpu.VMEM((DEVICES, COLS * ROWS, 128), BF)
    cols = pltpu.VMEM((COLS, DEVICES * ROWS, tokens), F32)
    square = pltpu.VMEM((COLS, 128, 128), BF)
    out, left_now, right_now = pl.pallas_call(
        functools.partial(adapter_kernel, step_size),
        out_shape=(
            jax.ShapeDtypeStruct((tokens, width), BF),
            jax.ShapeDtypeStruct(left_turned.shape, F32),
            jax.ShapeDtypeStruct(right_factor.shape, F32),
        ),
        in_specs=[vmem] * 4 + [pl.BlockSpec(memory_space=pl.ANY)] + [vmem] * 2,
        out_specs=(vmem, vmem, vmem),
        scratch_shapes=[
            pltpu.VMEM(frozen_weight_pairs.shape, BF),
            pltpu.VMEM((DEVICES, width, width), BF),
            pltpu.VMEM((2, DEVICES, tokens, width), BF),
            pltpu.VMEM((tokens, width), F32),
            pltpu.VMEM((tokens, width), F32),
            pltpu.VMEM((DEVICES, COLS * ROWS, width), F32),
            pltpu.VMEM((DEVICES, COLS * ROWS, width), BF),
            square,
            square,
            cols,
            cols,
            cols,
            small,
            small,
            small,
            small,
            pltpu.VMEM((2,) + slab, BF),
            pltpu.VMEM((2,) + slab, BF),
            pltpu.VMEM(slab, BF),
            pltpu.VMEM(slab, BF),
            pltpu.SemaphoreType.DMA,
            pltpu.SemaphoreType.DMA((len(PIECES) * PARTS, DEVICES, 4)),
            pltpu.SemaphoreType.DMA((len(PIECES) * PARTS, DEVICES)),
            pltpu.SemaphoreType.DMA((KINDS, DEVICES)),
            pltpu.SemaphoreType.DMA((KINDS, DEVICES)),
        ],
        compiler_params=pltpu.CompilerParams(
            collective_id=0, has_side_effects=True, vmem_limit_bytes=60 * 1024 * 1024
        ),
        name="adapter",
    )(
        x_first, target_first, x_second, target_second, frozen_weight_pairs, right_factor, left_turned
    )
    results = (out, left_now, right_now)
    out, left_now, right_now = pl.pallas_call(
        hand_over,
        out_shape=tuple(jax.ShapeDtypeStruct(a.shape, a.dtype) for a in results),
        in_specs=[vmem] * 3,
        out_specs=(vmem,) * 3,
        name="hand_over",
    )(*results)
    return (out, right_now, jnp.swapaxes(left_now, 1, 2))


def solution(mesh):
    fused = mesh.shape["tensor"] == DEVICES and mesh.shape["dp"] == 1
    body = fused_shards if fused else shards
    return jax.shard_map(
        body,
        mesh=mesh,
        in_specs=(
            P(("groups", "dp"), "tensor"),
            P(("groups", "dp"), "tensor"),
            P(("groups", "dp"), "tensor"),
            P(("groups", "dp"), "tensor"),
            P(None, "tensor"),
            P(("groups", "tensor"), None, None),
            P(("groups", "tensor"), None, None),
        ),
        out_specs=(
            P(("groups", "dp"), "tensor"),
            P(("groups", "tensor"), None, None),
            P(("groups", "tensor"), None, None),
        ),
        check_vma=False,
    )
```

```python
import functools

import jax
import jax.numpy as jnp
from jax import lax
from jax.experimental import pallas as pl
from jax.experimental.pallas import tpu as pltpu
from jax.sharding import PartitionSpec as P

MESH = pl.DeviceIdType.MESH
BF = jnp.bfloat16
F32 = jnp.float32
LANES = (((1,), (1,)), ((), ()))

exact_precision = lax.Precision.HIGHEST


def toward_blocks(buffer_rows):
    return lax.all_to_all(buffer_rows, "tensor", split_axis=0, concat_axis=1, tiled=True)


def toward_rows(buffer_blocks):
    return lax.all_to_all(buffer_blocks, "tensor", split_axis=1, concat_axis=0, tiled=True)


def rows_direct(buffer_rows):
    return lax.all_to_all(buffer_rows, "tensor", split_axis=0, concat_axis=1, tiled=True)


def blocks_direct(buffer_blocks):
    return lax.all_to_all(buffer_blocks, "tensor", split_axis=1, concat_axis=0, tiled=True)


def make_masks(rows_local, mesh_row_count, block_size):
    sub_count = mesh_row_count // block_size
    own_index = lax.axis_index("tensor") * rows_local + jnp.arange(rows_local, dtype=jnp.int32)
    positions = jnp.arange(sub_count, dtype=jnp.int32)
    block_mask = (positions[None, :] == (own_index % sub_count)[:, None]).astype(jnp.bfloat16)
    row_mask = (positions[:, None] == (own_index // block_size)[None, :]).astype(jnp.bfloat16)
    return (block_mask, row_mask)


def spread_rows(values, row_mask):
    block_size, rows_local, token_count = values.shape
    sub_count = row_mask.shape[0]
    spread = values[:, None, :, :] * row_mask[None, :, :, None]
    return spread.reshape(block_size * sub_count, rows_local, token_count)


def pick_block(received, block_mask):
    rows_local, mesh_row_count, token_count = received.shape
    sub_count = block_mask.shape[1]
    split = received.reshape(rows_local, sub_count, mesh_row_count // sub_count, token_count)
    return jnp.sum(split * block_mask[:, :, None, None], axis=1)


def spread_block(values, block_mask):
    rows_local, block_size, token_count = values.shape
    sub_count = block_mask.shape[1]
    spread = values[:, None, :, :] * block_mask[:, :, None, None]
    return spread.reshape(rows_local, sub_count * block_size, token_count)


def pick_rows(received, row_mask):
    mesh_row_count, rows_local, token_count = received.shape
    sub_count = row_mask.shape[0]
    split = received.reshape(mesh_row_count // sub_count, sub_count, rows_local, token_count)
    return jnp.sum(split * row_mask[None, :, :, None], axis=1)


def paired_product(segment, weight, block_size):
    token_count, width = segment.shape
    grid_local = weight.shape[1] // (2 * block_size)
    weight_rows = weight
    weight_rows = weight_rows.reshape(width // 2, grid_local, 2, block_size)
    pairs = segment.reshape(token_count, width // 2, 2)
    partial_value = jnp.einsum(
        "trs,rgsc->tgc", pairs, weight_rows, preferred_element_type=jnp.float32
    )
    return partial_value.reshape(token_count, grid_local * block_size)


def base_product(x_local, weight, block_size):
    return paired_product(lax.all_gather(x_local, "tensor", axis=1, tiled=True), weight, block_size)


def rows_to_block_side(values, masks_pair):
    return pick_block(rows_direct(spread_rows(values, masks_pair[1])), masks_pair[0])


def block_to_row_side(values, masks_pair):
    return pick_rows(blocks_direct(spread_block(values, masks_pair[0])), masks_pair[1])


def one_step(x_local, target, base_out, right_factor, left_factor, masks_pair, step_size):
    token_count = x_local.shape[0]
    rows_local = right_factor.shape[0]
    block_size = right_factor.shape[1]
    sub_count = left_factor.shape[1] // block_size
    upper_right_half = right_factor.astype(jnp.bfloat16)
    left_half = left_factor.astype(jnp.bfloat16)
    input_mesh_grid = x_local.reshape(token_count, rows_local, block_size)
    base_rows = base_out.reshape(token_count, rows_local, block_size).transpose(2, 1, 0)
    target_rows = (
        target.reshape(token_count, rows_local, block_size).transpose(2, 1, 0).astype(jnp.float32)
    )
    offset = (base_rows - target_rows).astype(jnp.bfloat16)
    hidden = jnp.einsum(
        "ves,esl->lev", input_mesh_grid, upper_right_half, preferred_element_type=jnp.float32
    ).astype(jnp.bfloat16)
    gathered = toward_blocks(jnp.repeat(hidden, sub_count, axis=0))
    mixed_out = jnp.einsum(
        "sit,sik->skt", gathered, left_half, preferred_element_type=jnp.float32
    ).astype(jnp.bfloat16)
    output_rows = None
    mixed_rows = block_to_row_side(mixed_out, masks_pair)
    output_rows = base_rows + mixed_rows.astype(jnp.float32)
    error_rows = (offset.astype(jnp.float32) + mixed_rows.astype(jnp.float32)).astype(jnp.bfloat16)
    error_blocks = rows_to_block_side(error_rows, masks_pair)
    left_grad = jnp.einsum(
        "sit,skt->sik", gathered, error_blocks, preferred_element_type=jnp.float32
    )
    back_terms = jnp.einsum(
        "skt,sik->sit", error_blocks, left_half, preferred_element_type=jnp.float32
    ).astype(jnp.bfloat16)
    returned = toward_rows(back_terms)
    hidden_gradient = jnp.sum(
        returned.reshape(block_size, sub_count, rows_local, token_count).astype(jnp.float32), axis=1
    )
    right_grad = jnp.einsum(
        "wfm,sfw->fms",
        input_mesh_grid.astype(jnp.float32),
        hidden_gradient,
        precision=exact_precision,
    )
    right_grad, left_grad = lax.psum((right_grad, left_grad), "dp")
    return (output_rows, right_factor - step_size * right_grad, left_factor - step_size * left_grad)


def shards(
    x_first, target_first, x_second, target_second, frozen_weight_pairs, right_factor, left_factor
):
    rows_local = right_factor.shape[0]
    block_size = right_factor.shape[1]
    token_count = x_first.shape[0]
    masks_pair = make_masks(rows_local, left_factor.shape[1], block_size)
    step_size = 1.0 / (token_count * lax.axis_size("dp"))
    base_first = base_product(x_first, frozen_weight_pairs, block_size)
    unused, right_now, left_now = one_step(
        x_first, target_first, base_first, right_factor, left_factor, masks_pair, step_size
    )
    base_second = base_product(x_second, frozen_weight_pairs, block_size)
    output_rows, right_now, left_now = one_step(
        x_second, target_second, base_second, right_now, left_now, masks_pair, step_size
    )
    result = (
        output_rows.transpose(2, 1, 0)
        .reshape(token_count, rows_local * block_size)
        .astype(jnp.bfloat16)
    )
    return (result, right_now, left_now)


Z_COUNT, DEVICES, ROWS, COLS = 4, 16, 8, 4
PIECES = ((0, 0, 384), (1, 0, 256), (1, 256, 128))
SUBS = ((0, 0, 192), (0, 192, 192), (1, 0, 128), (1, 128, 128), (1, 256, 128))
PIECE_SUBS = ((0, 1), (2, 3), (4,))
LAG = 1
RIGHT_IN, RIGHT_BACK, OFFSET, MIXED = 0, 1, 2, 2 + len(PIECES)
KINDS = 2 + 2 * len(PIECES)


def adapter_kernel(
    step_size, x1, t1, x2, t2, weight, right_in, left_in, out, left_out, right_out,
    w, wd, xg, acc, base, rgrad, rhalf, lhalf, lturn, hid, hgrad, mixed, right_send, right_recv,
    back_send, back_recv, off_send, off_recv, mix_send, mix_recv,
    w_sem, ag_send, ag_recv, a2a_send, a2a_recv,
):
    tokens, width = x1.shape
    half = width // 2
    me = lax.axis_index("tensor")
    z, x, core = me // 4, lax.rem(me // 2, 2), lax.rem(me, 2)
    x_peer = z * 4 + (1 - x) * 2 + core
    core_peer = z * 4 + x * 2 + (1 - core)

    w_copy = pltpu.make_async_copy(weight, w, w_sem)
    w_copy.start()

    barrier = pltpu.get_barrier_semaphore()

    @pl.loop(1, DEVICES)
    def _(n):
        pl.semaphore_signal(
            barrier, inc=1, device_id={"tensor": lax.rem(me + n, DEVICES)}, device_id_type=MESH
        )

    row_id = lax.broadcasted_iota(jnp.int32, (width, width), 0)
    col_id = lax.broadcasted_iota(jnp.int32, (width, width), 1)
    split = jnp.where(row_id == ((col_id & (half - 1)) << 1) + (col_id >> (half.bit_length() - 1)), 1.0, 0.0).astype(BF)
    xg[0, me] = jnp.dot(x1[...], split, preferred_element_type=F32).astype(BF)

    pl.semaphore_wait(barrier, DEVICES - 1)

    def exchange(kind, source, target, peer, cut):
        return pltpu.make_async_remote_copy(
            src_ref=source.at[peer, :, cut],
            dst_ref=target.at[me, :, cut],
            send_sem=a2a_send.at[kind, peer],
            recv_sem=a2a_recv.at[kind, me],
            device_id={"tensor": peer},
            device_id_type=MESH,
        )

    def landed(kind, target, peer, cut):
        return pltpu.make_async_remote_copy(
            src_ref=target.at[peer, :, cut],
            dst_ref=target.at[peer, :, cut],
            send_sem=a2a_send.at[kind, peer],
            recv_sem=a2a_recv.at[kind, peer],
            device_id={"tensor": peer},
            device_id_type=MESH,
        )

    def send_all(kind, source, target, cut):
        @pl.loop(1, DEVICES, unroll=5)
        def _(n):
            exchange(kind, source, target, lax.rem(me + n, DEVICES), cut).start()

        target[me, :, cut] = source[me, :, cut]

    def wait_all(kind, target, cut):
        @pl.loop(1, DEVICES, unroll=5)
        def _(n):
            landed(kind, target, lax.rem(me + n, DEVICES), cut).wait_recv()

    def sent_all(kind, source, target, cut):
        @pl.loop(1, DEVICES)
        def _(n):
            exchange(kind, source, target, lax.rem(me + n, DEVICES), cut).wait_send()

    def span(piece):
        return slice(PIECES[piece][1], PIECES[piece][1] + PIECES[piece][2])

    def hop(sub, chunk, direction, peer):
        b, first, count = SUBS[sub]
        return pltpu.make_async_remote_copy(
            src_ref=xg.at[b, chunk, first : first + count],
            dst_ref=xg.at[b, chunk, first : first + count],
            send_sem=ag_send.at[sub, chunk, direction],
            recv_sem=ag_recv.at[sub, chunk],
            device_id={"tensor": peer},
            device_id_type=MESH,
        )

    def z_order(k):
        high = z // 2
        mirrored = z * (1 - high) + (3 - z) * high
        order = k + (1 - k // 2) * mirrored * (1 - 2 * k)
        return order * (1 - high) + (3 - order) * high

    def along_z(sub, source_z, act):
        chunk = source_z * 4 + x * 2 + core

        @pl.when((source_z <= z) & (z < Z_COUNT - 1))
        def _():
            act(hop(sub, chunk, 0, me + 4))

        @pl.when((source_z >= z) & (z > 0))
        def _():
            act(hop(sub, chunk, 1, me - 4))

    def across(sub, source_z, act):
        chunk = source_z * 4 + x * 2 + core
        act(hop(sub, chunk, 2, x_peer))
        act(hop(sub, chunk, 3, core_peer))

    def start(copy):
        copy.start()

    def apply_base(piece, chunk):
        b, cut = PIECES[piece][0], span(piece)
        acc[cut, :] += jnp.dot(xg[b, chunk, cut, :], wd[chunk], preferred_element_type=F32)

    def apply_hidden(piece, chunk):
        b, cut = PIECES[piece][0], span(piece)
        value = lax.dot_general(
            rhalf[chunk], xg[b, chunk, cut, :], LANES, preferred_element_type=F32
        )
        for d in range(COLS):
            hid[d, pl.ds(pl.multiple_of(chunk * ROWS, ROWS), ROWS), cut] = value[
                d * ROWS : (d + 1) * ROWS
            ]

    def landed_all(piece, chunk):
        for sub in PIECE_SUBS[piece]:
            hop(sub, chunk, 3, core_peer).wait_recv()

    def use(piece, chunk, with_hidden):
        apply_base(piece, chunk)
        if with_hidden:
            apply_hidden(piece, chunk)

    def use_own(piece, k, with_hidden):
        def one(m, carry):
            chunk = z_order(k) * 4 + x * 2 + core + m * (1 - 2 * core)

            @pl.when(m > 0)
            def _():
                landed_all(piece, chunk)

            use(piece, chunk, with_hidden)
            return carry

        lax.fori_loop(0, 2, one, 0, unroll=True)

    def use_other(piece, k, with_hidden):
        def one(m, carry):
            chunk = z_order(k) * 4 + (1 - x) * 2 + core + m * (1 - 2 * core)

            @pl.when(m > 0)
            def _():
                landed_all(piece, chunk)

            use(piece, chunk, with_hidden)
            return carry

        lax.fori_loop(0, 2, one, 0, unroll=True)

    def from_z(sub, k):
        next_z = z_order(k)
        hop(sub, next_z * 4 + x * 2 + core, 3, core_peer).wait_recv()
        along_z(sub, next_z, start)
        across(sub, next_z, start)

    def from_x(sub, k):
        copy = hop(sub, z_order(k) * 4 + (1 - x) * 2 + core, 3, core_peer)
        copy.wait_recv()
        copy.start()

    def gather_first(first, last, with_hidden):
        def body(k, carry):
            @pl.when(k < 3)
            def _():
                from_z(0, k + 1)

            @pl.when(k == 3)
            def _():
                across(2, z, start)
                across(3, z, start)

            from_x(0, k)

            @pl.when(k > 0)
            def _():
                use_other(0, k - 1, with_hidden)

            @pl.when(k < 3)
            def _():
                from_z(1, k + 1)

            @pl.when(k == 2)
            def _():
                along_z(2, z, start)
                along_z(3, z, start)

            from_x(1, k)
            use_own(0, k, with_hidden)
            return carry

        lax.fori_loop(first, last, body, 0)
        if last == 4:
            use_other(0, 3, with_hidden)

    def gather_rest(first, last, with_hidden):
        def body(k, carry):
            @pl.when(k < 3)
            def _():
                from_z(2, k + 1)

            from_x(2, k)

            @pl.when(k > 0)
            def _():
                use_other(1, k - 1, with_hidden)

            @pl.when(k < 3)
            def _():
                from_z(3, k + 1)

            @pl.when(k == LAG - 1)
            def _():
                along_z(4, z, start)
                across(4, z, start)

            @pl.when(k >= LAG)
            def _():
                from_z(4, k - LAG + 1)

            from_x(3, k)
            use_own(1, k, with_hidden)

            @pl.when(k >= LAG)
            def _():
                from_x(4, k - LAG)

                @pl.when(k > LAG)
                def _():
                    use_other(2, k - LAG - 1, with_hidden)

                use_own(2, k - LAG, with_hidden)

            return carry

        lax.fori_loop(first, last, body, 0)

    def sent_gather(sub):
        @pl.loop(0, Z_COUNT)
        def _(source_z):
            along_z(sub, source_z, lambda copy: copy.wait_send())
            across(sub, source_z, lambda copy: copy.wait_send())
            hop(sub, source_z * 4 + (1 - x) * 2 + core, 3, core_peer).wait_send()

    def clear(piece):
        acc[span(piece), :] = jnp.zeros((PIECES[piece][2], width), F32)

    def finish_base(piece, target):
        b, cut, count = PIECES[piece][0], span(piece), PIECES[piece][2]
        value = acc[cut, :]
        if b == 1:
            base[cut, :] = value
        offset = (value - target[cut, :].astype(F32)).astype(BF)
        turned = lax.dot_general(turn, offset, LANES, preferred_element_type=F32)
        off_send[b, :, :, cut] = turned.astype(BF).reshape(DEVICES, COLS * ROWS, count)
        send_all(OFFSET + piece, off_send.at[b], off_recv.at[b], cut)

    def take_left(ref):
        for d in range(COLS):
            pair = jnp.concatenate([ref[2 * d], ref[2 * d + 1]], axis=0)
            lturn[d] = pair.astype(BF)
            lhalf[d] = pair.T.astype(BF)

    def mix(piece):
        cut = span(piece)
        for d in range(COLS):
            mixed[d, :, cut] = (
                jnp.dot(lturn[d], hid[d, :, cut].astype(BF), preferred_element_type=F32)
                .astype(BF)
                .astype(F32)
            )

    def send_mixed(piece):
        cut, count = span(piece), PIECES[piece][2]
        stacked = jnp.stack(
            [mixed[d, :, cut].reshape(DEVICES, ROWS, count) for d in range(COLS)], axis=1
        )
        mix_send[:, :, cut] = stacked.reshape(DEVICES, COLS * ROWS, count).astype(BF)
        send_all(MIXED + piece, mix_send, mix_recv, cut)

    block_row = lax.broadcasted_iota(jnp.int32, (COLS * ROWS, width), 0)
    block_col = lax.broadcasted_iota(jnp.int32, (COLS * ROWS, width), 1)
    on_block = lax.rem(block_row, ROWS) == lax.rem(block_col, half) // (half // ROWS)

    def step_left(piece, d, error):
        cut = span(piece)
        grad = step_size * lax.dot_general(
            error, hid[d, :, cut].astype(BF), LANES, preferred_element_type=F32
        )
        left_out[2 * d] = left_out[2 * d] - grad[:64]
        left_out[2 * d + 1] = left_out[2 * d + 1] - grad[64:]

    def backward(piece, later):
        b, cut, count = PIECES[piece][0], span(piece), PIECES[piece][2]
        wait_all(OFFSET + piece, off_recv.at[b], cut)
        received = off_recv[b, :, :, cut].astype(F32).reshape(DEVICES, COLS, ROWS, count)
        errors = []
        for d in range(COLS):
            offset = received[:, d].reshape(DEVICES * ROWS, count)
            error = (offset + mixed[d, :, cut]).astype(BF)
            hgrad[d, :, cut] = jnp.dot(lhalf[d], error, preferred_element_type=F32)
            if later:
                errors.append(error)
            else:
                step_left(piece, d, error)

        @pl.loop(0, DEVICES, unroll=4)
        def _(chunk):
            rows = pl.ds(pl.multiple_of(chunk * ROWS, ROWS), ROWS)
            left = jnp.concatenate([hgrad[d, rows, cut] for d in range(COLS)], axis=0).astype(BF)
            grad = jnp.dot(left, xg[b, chunk, cut, :], preferred_element_type=F32)
            rgrad[chunk] = rgrad[chunk] + jnp.where(on_block, grad, 0.0)

        return errors

    small_lane = lax.broadcasted_iota(jnp.int32, (COLS * ROWS, 128), 1)

    def take_right():
        @pl.loop(0, DEVICES, unroll=4)
        def _(chunk):
            value = right_recv[chunk].astype(F32)
            turned = pltpu.roll(value, 64, 1)
            even = jnp.where(small_lane < 64, value, turned)
            odd = jnp.where(small_lane < 64, turned, value)
            full = jnp.where(on_block, jnp.concatenate([even, even, odd, odd], axis=1), 0.0)
            rhalf[chunk] = (full - step_size * rgrad[chunk]).astype(BF)

    def give_output(piece):
        cut, count = span(piece), PIECES[piece][2]
        wait_all(MIXED + piece, mix_recv, cut)
        rows_in = mix_recv[:, :, cut].reshape(DEVICES * COLS * ROWS, count).astype(F32)
        mixed_rows = jnp.dot(rows_in.T.astype(BF), turn, preferred_element_type=F32)
        out[cut, :] = (base[cut, :] + mixed_rows).astype(BF)

    for sub in PIECE_SUBS[0]:
        along_z(sub, z, start)
        across(sub, z, start)

    block_id = lax.broadcasted_iota(jnp.int32, (64, 128), 0)
    lane_id = lax.broadcasted_iota(jnp.int32, (64, 128), 1)
    own_lane = block_id == 2 * lax.rem(lane_id, 32) + lane_id // 64
    pairs = jnp.where(own_lane, 1.0, 0.0).astype(BF)
    one_pair = jnp.where(own_lane & (lax.rem(lane_id, 64) < 32), 1.0, 0.0).astype(BF)
    spread = [
        jnp.dot(right_in[i].T.astype(BF), pairs, preferred_element_type=F32) for i in range(ROWS)
    ]
    right_send[...] = (
        jnp.stack(spread, axis=1).reshape(DEVICES, COLS * ROWS, 128).astype(BF)
    )
    lanes = slice(0, 128)
    send_all(RIGHT_IN, right_send, right_recv, lanes)

    xg[1, me] = jnp.dot(x2[...], split, preferred_element_type=F32).astype(BF)
    turn = jnp.where(
        col_id == ((row_id & (ROWS - 1)) * (width // ROWS)) + (row_id >> (ROWS.bit_length() - 1)), 1.0, 0.0
    ).astype(BF)
    rgrad[...] = jnp.zeros_like(rgrad)
    left_out[...] = left_in[...]
    take_left(left_in)
    clear(0)
    w_copy.wait()
    low = lax.broadcasted_iota(jnp.int32, (half, 128), 1) < 64

    @pl.loop(0, DEVICES)
    def _(chunk):
        rows = pl.ds(pl.multiple_of(chunk * half, half), half)
        for n in range(width // 128):
            first = w[rows, 256 * n : 256 * n + 128]
            second = w[rows, 256 * n + 128 : 256 * n + 256]
            lanes_n = slice(128 * n, 128 * n + 128)
            wd[chunk, :half, lanes_n] = jnp.concatenate([first[:, :64], second[:, :64]], axis=1)
            wd[chunk, half:, lanes_n] = jnp.concatenate([first[:, 64:], second[:, 64:]], axis=1)


    def early(piece, steps):
        def one(m, carry):
            apply_hidden(piece, z_order(m // 4) * 4 + lax.rem(x * 2 + lax.rem(m, 4), 4))
            return carry

        if steps > 0:
            lax.fori_loop(0, 4 * steps - 2, one, 0)

    gather_first(0, 2, False)
    wait_all(RIGHT_IN, right_recv, lanes)
    take_right()
    early(0, 2)
    gather_first(2, 4, True)
    finish_base(0, t1)
    clear(1)
    clear(2)
    mix(0)
    gather_rest(0, 3, False)
    backward(0, False)
    take_left(left_out)
    take_right()
    early(1, 3)
    early(2, 3 - LAG)
    gather_rest(3, 4, True)
    use_other(1, 3, True)
    finish_base(1, t2)
    mix(1)
    send_mixed(1)
    from_x(4, 3)
    use_other(2, 2, True)
    use_own(2, 3, True)
    use_other(2, 3, True)
    finish_base(2, t2)
    mix(2)
    send_mixed(2)
    backward(1, False)
    give_output(1)
    errors = backward(2, True)

    @pl.loop(0, DEVICES, unroll=4)
    def _(chunk):
        value = rgrad[chunk]
        folded = []
        for s in range(2):
            part = value[:, s * half : s * half + 128] + value[:, s * half + 128 : (s + 1) * half]
            part = part + pltpu.roll(part, 64, 1)
            folded.append(part + pltpu.roll(part, 32, 1))
        back_send[chunk] = jnp.where(small_lane < 64, folded[0], folded[1]).astype(BF)

    send_all(RIGHT_BACK, back_send, back_recv, lanes)
    for d in range(COLS):
        step_left(2, d, errors[d])
    give_output(2)
    for sub in range(len(SUBS)):
        sent_gather(sub)
    for piece in range(len(PIECES)):
        b = PIECES[piece][0]
        sent_all(OFFSET + piece, off_send.at[b], off_recv.at[b], span(piece))
        if b == 1:
            sent_all(MIXED + piece, mix_send, mix_recv, span(piece))
    sent_all(RIGHT_IN, right_send, right_recv, lanes)
    wait_all(RIGHT_BACK, back_recv, lanes)
    returned = back_recv[...].astype(F32).reshape(DEVICES * COLS, ROWS, 128)
    for i in range(ROWS):
        grad = lax.dot_general(
            one_pair, returned[:, i, :].astype(BF), LANES, preferred_element_type=F32
        )
        right_out[i] = right_in[i] - step_size * grad

    sent_all(RIGHT_BACK, back_send, back_recv, lanes)


def hand_over(out, left, right, out_to, left_to, right_to):
    out_to[...] = out[...]
    left_to[...] = left[...]
    right_to[...] = right[...]


def fused_shards(
    x_first, target_first, x_second, target_second, frozen_weight_pairs, right_factor, left_factor
):
    tokens, width = x_first.shape
    step_size = 1.0 / tokens
    left_turned = jnp.swapaxes(left_factor, 1, 2)
    vmem = pl.BlockSpec(memory_space=pltpu.VMEM)
    slab = (DEVICES, COLS * ROWS, tokens)
    small = pltpu.VMEM((DEVICES, COLS * ROWS, 128), BF)
    cols = pltpu.VMEM((COLS, DEVICES * ROWS, tokens), F32)
    square = pltpu.VMEM((COLS, 128, 128), BF)
    out, left_now, right_now = pl.pallas_call(
        functools.partial(adapter_kernel, step_size),
        out_shape=(
            jax.ShapeDtypeStruct((tokens, width), BF),
            jax.ShapeDtypeStruct(left_turned.shape, F32),
            jax.ShapeDtypeStruct(right_factor.shape, F32),
        ),
        in_specs=[vmem] * 4 + [pl.BlockSpec(memory_space=pl.ANY)] + [vmem] * 2,
        out_specs=(vmem, vmem, vmem),
        scratch_shapes=[
            pltpu.VMEM(frozen_weight_pairs.shape, BF),
            pltpu.VMEM((DEVICES, width, width), BF),
            pltpu.VMEM((2, DEVICES, tokens, width), BF),
            pltpu.VMEM((tokens, width), F32),
            pltpu.VMEM((tokens, width), F32),
            pltpu.VMEM((DEVICES, COLS * ROWS, width), F32),
            pltpu.VMEM((DEVICES, COLS * ROWS, width), BF),
            square,
            square,
            cols,
            cols,
            cols,
            small,
            small,
            small,
            small,
            pltpu.VMEM((2,) + slab, BF),
            pltpu.VMEM((2,) + slab, BF),
            pltpu.VMEM(slab, BF),
            pltpu.VMEM(slab, BF),
            pltpu.SemaphoreType.DMA,
            pltpu.SemaphoreType.DMA((len(SUBS), DEVICES, 4)),
            pltpu.SemaphoreType.DMA((len(SUBS), DEVICES)),
            pltpu.SemaphoreType.DMA((KINDS, DEVICES)),
            pltpu.SemaphoreType.DMA((KINDS, DEVICES)),
        ],
        compiler_params=pltpu.CompilerParams(
            collective_id=0, has_side_effects=True, vmem_limit_bytes=60 * 1024 * 1024
        ),
        name="adapter",
    )(
        x_first, target_first, x_second, target_second, frozen_weight_pairs, right_factor, left_turned
    )
    results = (out, left_now, right_now)
    out, left_now, right_now = pl.pallas_call(
        hand_over,
        out_shape=tuple(jax.ShapeDtypeStruct(a.shape, a.dtype) for a in results),
        in_specs=[vmem] * 3,
        out_specs=(vmem,) * 3,
        name="hand_over",
    )(*results)
    return (out, right_now, jnp.swapaxes(left_now, 1, 2))


def solution(mesh):
    fused = mesh.shape["tensor"] == DEVICES and mesh.shape["dp"] == 1
    body = fused_shards if fused else shards
    return jax.shard_map(
        body,
        mesh=mesh,
        in_specs=(
            P(("groups", "dp"), "tensor"),
            P(("groups", "dp"), "tensor"),
            P(("groups", "dp"), "tensor"),
            P(("groups", "dp"), "tensor"),
            P(None, "tensor"),
            P(("groups", "tensor"), None, None),
            P(("groups", "tensor"), None, None),
        ),
        out_specs=(
            P(("groups", "dp"), "tensor"),
            P(("groups", "tensor"), None, None),
            P(("groups", "tensor"), None, None),
        ),
        check_vma=False,
    )
```

```python
import functools

import jax
import jax.numpy as jnp
from jax import lax
from jax.experimental import pallas as pl
from jax.experimental.pallas import tpu as pltpu
from jax.sharding import PartitionSpec as P

MESH = pl.DeviceIdType.MESH
BF = jnp.bfloat16
F32 = jnp.float32
LANES = (((1,), (1,)), ((), ()))

exact_precision = lax.Precision.HIGHEST


def toward_blocks(buffer_rows):
    return lax.all_to_all(buffer_rows, "tensor", split_axis=0, concat_axis=1, tiled=True)


def toward_rows(buffer_blocks):
    return lax.all_to_all(buffer_blocks, "tensor", split_axis=1, concat_axis=0, tiled=True)


def rows_direct(buffer_rows):
    return lax.all_to_all(buffer_rows, "tensor", split_axis=0, concat_axis=1, tiled=True)


def blocks_direct(buffer_blocks):
    return lax.all_to_all(buffer_blocks, "tensor", split_axis=1, concat_axis=0, tiled=True)


def make_masks(rows_local, mesh_row_count, block_size):
    sub_count = mesh_row_count // block_size
    own_index = lax.axis_index("tensor") * rows_local + jnp.arange(rows_local, dtype=jnp.int32)
    positions = jnp.arange(sub_count, dtype=jnp.int32)
    block_mask = (positions[None, :] == (own_index % sub_count)[:, None]).astype(jnp.bfloat16)
    row_mask = (positions[:, None] == (own_index // block_size)[None, :]).astype(jnp.bfloat16)
    return (block_mask, row_mask)


def spread_rows(values, row_mask):
    block_size, rows_local, token_count = values.shape
    sub_count = row_mask.shape[0]
    spread = values[:, None, :, :] * row_mask[None, :, :, None]
    return spread.reshape(block_size * sub_count, rows_local, token_count)


def pick_block(received, block_mask):
    rows_local, mesh_row_count, token_count = received.shape
    sub_count = block_mask.shape[1]
    split = received.reshape(rows_local, sub_count, mesh_row_count // sub_count, token_count)
    return jnp.sum(split * block_mask[:, :, None, None], axis=1)


def spread_block(values, block_mask):
    rows_local, block_size, token_count = values.shape
    sub_count = block_mask.shape[1]
    spread = values[:, None, :, :] * block_mask[:, :, None, None]
    return spread.reshape(rows_local, sub_count * block_size, token_count)


def pick_rows(received, row_mask):
    mesh_row_count, rows_local, token_count = received.shape
    sub_count = row_mask.shape[0]
    split = received.reshape(mesh_row_count // sub_count, sub_count, rows_local, token_count)
    return jnp.sum(split * row_mask[None, :, :, None], axis=1)


def paired_product(segment, weight, block_size):
    token_count, width = segment.shape
    grid_local = weight.shape[1] // (2 * block_size)
    weight_rows = weight
    weight_rows = weight_rows.reshape(width // 2, grid_local, 2, block_size)
    pairs = segment.reshape(token_count, width // 2, 2)
    partial_value = jnp.einsum(
        "trs,rgsc->tgc", pairs, weight_rows, preferred_element_type=jnp.float32
    )
    return partial_value.reshape(token_count, grid_local * block_size)


def base_product(x_local, weight, block_size):
    return paired_product(lax.all_gather(x_local, "tensor", axis=1, tiled=True), weight, block_size)


def rows_to_block_side(values, masks_pair):
    return pick_block(rows_direct(spread_rows(values, masks_pair[1])), masks_pair[0])


def block_to_row_side(values, masks_pair):
    return pick_rows(blocks_direct(spread_block(values, masks_pair[0])), masks_pair[1])


def one_step(x_local, target, base_out, right_factor, left_factor, masks_pair, step_size):
    token_count = x_local.shape[0]
    rows_local = right_factor.shape[0]
    block_size = right_factor.shape[1]
    sub_count = left_factor.shape[1] // block_size
    upper_right_half = right_factor.astype(jnp.bfloat16)
    left_half = left_factor.astype(jnp.bfloat16)
    input_mesh_grid = x_local.reshape(token_count, rows_local, block_size)
    base_rows = base_out.reshape(token_count, rows_local, block_size).transpose(2, 1, 0)
    target_rows = (
        target.reshape(token_count, rows_local, block_size).transpose(2, 1, 0).astype(jnp.float32)
    )
    offset = (base_rows - target_rows).astype(jnp.bfloat16)
    hidden = jnp.einsum(
        "ves,esl->lev", input_mesh_grid, upper_right_half, preferred_element_type=jnp.float32
    ).astype(jnp.bfloat16)
    gathered = toward_blocks(jnp.repeat(hidden, sub_count, axis=0))
    mixed_out = jnp.einsum(
        "sit,sik->skt", gathered, left_half, preferred_element_type=jnp.float32
    ).astype(jnp.bfloat16)
    output_rows = None
    mixed_rows = block_to_row_side(mixed_out, masks_pair)
    output_rows = base_rows + mixed_rows.astype(jnp.float32)
    error_rows = (offset.astype(jnp.float32) + mixed_rows.astype(jnp.float32)).astype(jnp.bfloat16)
    error_blocks = rows_to_block_side(error_rows, masks_pair)
    left_grad = jnp.einsum(
        "sit,skt->sik", gathered, error_blocks, preferred_element_type=jnp.float32
    )
    back_terms = jnp.einsum(
        "skt,sik->sit", error_blocks, left_half, preferred_element_type=jnp.float32
    ).astype(jnp.bfloat16)
    returned = toward_rows(back_terms)
    hidden_gradient = jnp.sum(
        returned.reshape(block_size, sub_count, rows_local, token_count).astype(jnp.float32), axis=1
    )
    right_grad = jnp.einsum(
        "wfm,sfw->fms",
        input_mesh_grid.astype(jnp.float32),
        hidden_gradient,
        precision=exact_precision,
    )
    right_grad, left_grad = lax.psum((right_grad, left_grad), "dp")
    return (output_rows, right_factor - step_size * right_grad, left_factor - step_size * left_grad)


def shards(
    x_first, target_first, x_second, target_second, frozen_weight_pairs, right_factor, left_factor
):
    rows_local = right_factor.shape[0]
    block_size = right_factor.shape[1]
    token_count = x_first.shape[0]
    masks_pair = make_masks(rows_local, left_factor.shape[1], block_size)
    step_size = 1.0 / (token_count * lax.axis_size("dp"))
    base_first = base_product(x_first, frozen_weight_pairs, block_size)
    unused, right_now, left_now = one_step(
        x_first, target_first, base_first, right_factor, left_factor, masks_pair, step_size
    )
    base_second = base_product(x_second, frozen_weight_pairs, block_size)
    output_rows, right_now, left_now = one_step(
        x_second, target_second, base_second, right_now, left_now, masks_pair, step_size
    )
    result = (
        output_rows.transpose(2, 1, 0)
        .reshape(token_count, rows_local * block_size)
        .astype(jnp.bfloat16)
    )
    return (result, right_now, left_now)


Z_COUNT, DEVICES, ROWS, COLS = 4, 16, 8, 4
PIECES = ((0, 0, 384), (1, 0, 256), (1, 256, 128))
SUBS = ((0, 0, 192), (0, 192, 192), (1, 0, 128), (1, 128, 128), (1, 256, 128))
PIECE_SUBS = ((0, 1), (2, 3), (4,))
LAG = 1
RIGHT_IN, RIGHT_BACK, OFFSET, MIXED = 0, 1, 2, 2 + len(PIECES)
KINDS = 2 + 2 * len(PIECES)


def adapter_kernel(
    step_size, x1, t1, x2, t2, weight, right_in, left_in, out, left_out, right_out,
    w, wd, xg, acc, base, rgrad, rhalf, lhalf, lturn, hid, hgrad, mixed, right_send, right_recv,
    back_send, back_recv, off_send, off_recv, mix_send, mix_recv,
    w_sem, ag_send, ag_recv, a2a_send, a2a_recv,
):
    tokens, width = x1.shape
    half = width // 2
    me = lax.axis_index("tensor")
    z, x, core = me // 4, lax.rem(me // 2, 2), lax.rem(me, 2)
    x_peer = z * 4 + (1 - x) * 2 + core
    core_peer = z * 4 + x * 2 + (1 - core)

    w_copy = pltpu.make_async_copy(weight, w, w_sem)
    w_copy.start()

    barrier = pltpu.get_barrier_semaphore()

    @pl.loop(1, DEVICES)
    def _(n):
        pl.semaphore_signal(
            barrier, inc=1, device_id={"tensor": lax.rem(me + n, DEVICES)}, device_id_type=MESH
        )

    row_id = lax.broadcasted_iota(jnp.int32, (width, width), 0)
    col_id = lax.broadcasted_iota(jnp.int32, (width, width), 1)
    split = jnp.where(row_id == ((col_id & (half - 1)) << 1) + (col_id >> (half.bit_length() - 1)), 1.0, 0.0).astype(BF)
    xg[0, me] = jnp.dot(x1[...], split, preferred_element_type=F32).astype(BF)

    pl.semaphore_wait(barrier, DEVICES - 1)

    def exchange(kind, source, target, peer, cut):
        return pltpu.make_async_remote_copy(
            src_ref=source.at[peer, :, cut],
            dst_ref=target.at[me, :, cut],
            send_sem=a2a_send.at[kind, peer],
            recv_sem=a2a_recv.at[kind, me],
            device_id={"tensor": peer},
            device_id_type=MESH,
        )

    def landed(kind, target, peer, cut):
        return pltpu.make_async_remote_copy(
            src_ref=target.at[peer, :, cut],
            dst_ref=target.at[peer, :, cut],
            send_sem=a2a_send.at[kind, peer],
            recv_sem=a2a_recv.at[kind, peer],
            device_id={"tensor": peer},
            device_id_type=MESH,
        )

    def send_all(kind, source, target, cut):
        @pl.loop(1, DEVICES, unroll=5)
        def _(n):
            exchange(kind, source, target, lax.rem(me + n, DEVICES), cut).start()

        target[me, :, cut] = source[me, :, cut]

    def wait_all(kind, target, cut):
        @pl.loop(1, DEVICES, unroll=5)
        def _(n):
            landed(kind, target, lax.rem(me + n, DEVICES), cut).wait_recv()

    def sent_all(kind, source, target, cut):
        @pl.loop(1, DEVICES)
        def _(n):
            exchange(kind, source, target, lax.rem(me + n, DEVICES), cut).wait_send()

    def span(piece):
        return slice(PIECES[piece][1], PIECES[piece][1] + PIECES[piece][2])

    def hop(sub, chunk, direction, peer):
        b, first, count = SUBS[sub]
        return pltpu.make_async_remote_copy(
            src_ref=xg.at[b, chunk, first : first + count],
            dst_ref=xg.at[b, chunk, first : first + count],
            send_sem=ag_send.at[sub, chunk, direction],
            recv_sem=ag_recv.at[sub, chunk],
            device_id={"tensor": peer},
            device_id_type=MESH,
        )

    def z_order(k):
        high = z // 2
        mirrored = z * (1 - high) + (3 - z) * high
        order = k + (1 - k // 2) * mirrored * (1 - 2 * k)
        return order * (1 - high) + (3 - order) * high

    def along_z(sub, source_z, act):
        chunk = source_z * 4 + x * 2 + core

        @pl.when((source_z <= z) & (z < Z_COUNT - 1))
        def _():
            act(hop(sub, chunk, 0, me + 4))

        @pl.when((source_z >= z) & (z > 0))
        def _():
            act(hop(sub, chunk, 1, me - 4))

    def across(sub, source_z, act):
        chunk = source_z * 4 + x * 2 + core
        act(hop(sub, chunk, 2, x_peer))
        act(hop(sub, chunk, 3, core_peer))

    def start(copy):
        copy.start()

    def apply_base(piece, chunk):
        b, cut = PIECES[piece][0], span(piece)
        acc[cut, :] += jnp.dot(xg[b, chunk, cut, :], wd[chunk], preferred_element_type=F32)

    def apply_hidden(piece, chunk):
        b, cut = PIECES[piece][0], span(piece)
        value = lax.dot_general(
            rhalf[chunk], xg[b, chunk, cut, :], LANES, preferred_element_type=F32
        )
        for d in range(COLS):
            hid[d, pl.ds(pl.multiple_of(chunk * ROWS, ROWS), ROWS), cut] = value[
                d * ROWS : (d + 1) * ROWS
            ]

    def landed_all(piece, chunk):
        for sub in PIECE_SUBS[piece]:
            hop(sub, chunk, 3, core_peer).wait_recv()

    def use(piece, chunk, with_hidden):
        apply_base(piece, chunk)
        if with_hidden:
            apply_hidden(piece, chunk)

    def use_own(piece, k, with_hidden):
        def one(m, carry):
            chunk = z_order(k) * 4 + x * 2 + core + m * (1 - 2 * core)

            @pl.when(m > 0)
            def _():
                landed_all(piece, chunk)

            use(piece, chunk, with_hidden)
            return carry

        lax.fori_loop(0, 2, one, 0, unroll=True)

    def use_other(piece, k, with_hidden):
        def one(m, carry):
            chunk = z_order(k) * 4 + (1 - x) * 2 + core + m * (1 - 2 * core)

            @pl.when(m > 0)
            def _():
                landed_all(piece, chunk)

            use(piece, chunk, with_hidden)
            return carry

        lax.fori_loop(0, 2, one, 0, unroll=True)

    def from_z(sub, k):
        next_z = z_order(k)
        hop(sub, next_z * 4 + x * 2 + core, 3, core_peer).wait_recv()
        along_z(sub, next_z, start)
        across(sub, next_z, start)

    def from_x(sub, k):
        copy = hop(sub, z_order(k) * 4 + (1 - x) * 2 + core, 3, core_peer)
        copy.wait_recv()
        copy.start()

    def gather_first(first, last, with_hidden):
        def body(k, carry):
            @pl.when(k < 3)
            def _():
                from_z(0, k + 1)

            @pl.when(k == 3)
            def _():
                across(2, z, start)
                across(3, z, start)

            from_x(0, k)

            @pl.when(k < 3)
            def _():
                from_z(1, k + 1)

            @pl.when(k > 0)
            def _():
                use_other(0, k - 1, with_hidden)

            @pl.when(k == 2)
            def _():
                along_z(2, z, start)
                along_z(3, z, start)

            from_x(1, k)
            use_own(0, k, with_hidden)
            return carry

        lax.fori_loop(first, last, body, 0)
        if last == 4:
            use_other(0, 3, with_hidden)

    def gather_rest(first, last, with_hidden):
        def body(k, carry):
            @pl.when(k < 3)
            def _():
                from_z(2, k + 1)

            from_x(2, k)

            @pl.when(k < 3)
            def _():
                from_z(3, k + 1)

            @pl.when(k > 0)
            def _():
                use_other(1, k - 1, with_hidden)

            @pl.when(k == LAG - 1)
            def _():
                along_z(4, z, start)
                across(4, z, start)

            @pl.when(k >= LAG)
            def _():
                from_z(4, k - LAG + 1)

            from_x(3, k)
            use_own(1, k, with_hidden)

            @pl.when(k >= LAG)
            def _():
                from_x(4, k - LAG)

                @pl.when(k > LAG)
                def _():
                    use_other(2, k - LAG - 1, with_hidden)

                use_own(2, k - LAG, with_hidden)

            return carry

        lax.fori_loop(first, last, body, 0)

    def sent_gather(sub):
        @pl.loop(0, Z_COUNT)
        def _(source_z):
            along_z(sub, source_z, lambda copy: copy.wait_send())
            across(sub, source_z, lambda copy: copy.wait_send())
            hop(sub, source_z * 4 + (1 - x) * 2 + core, 3, core_peer).wait_send()

    def clear(piece):
        acc[span(piece), :] = jnp.zeros((PIECES[piece][2], width), F32)

    def finish_base(piece, target):
        b, cut, count = PIECES[piece][0], span(piece), PIECES[piece][2]
        value = acc[cut, :]
        if b == 1:
            base[cut, :] = value
        offset = (value - target[cut, :].astype(F32)).astype(BF)
        turned = lax.dot_general(turn, offset, LANES, preferred_element_type=F32)
        off_send[b, :, :, cut] = turned.astype(BF).reshape(DEVICES, COLS * ROWS, count)
        send_all(OFFSET + piece, off_send.at[b], off_recv.at[b], cut)

    def take_left(ref):
        for d in range(COLS):
            pair = jnp.concatenate([ref[2 * d], ref[2 * d + 1]], axis=0)
            lturn[d] = pair.astype(BF)
            lhalf[d] = pair.T.astype(BF)

    def mix(piece):
        cut = span(piece)
        for d in range(COLS):
            mixed[d, :, cut] = (
                jnp.dot(lturn[d], hid[d, :, cut].astype(BF), preferred_element_type=F32)
                .astype(BF)
                .astype(F32)
            )

    def send_mixed(piece):
        cut, count = span(piece), PIECES[piece][2]
        stacked = jnp.stack(
            [mixed[d, :, cut].reshape(DEVICES, ROWS, count) for d in range(COLS)], axis=1
        )
        mix_send[:, :, cut] = stacked.reshape(DEVICES, COLS * ROWS, count).astype(BF)
        send_all(MIXED + piece, mix_send, mix_recv, cut)

    block_row = lax.broadcasted_iota(jnp.int32, (COLS * ROWS, width), 0)
    block_col = lax.broadcasted_iota(jnp.int32, (COLS * ROWS, width), 1)
    on_block = lax.rem(block_row, ROWS) == lax.rem(block_col, half) // (half // ROWS)

    def step_left(piece, d, error):
        cut = span(piece)
        grad = step_size * lax.dot_general(
            error, hid[d, :, cut].astype(BF), LANES, preferred_element_type=F32
        )
        left_out[2 * d] = left_out[2 * d] - grad[:64]
        left_out[2 * d + 1] = left_out[2 * d + 1] - grad[64:]

    def backward(piece, later):
        b, cut, count = PIECES[piece][0], span(piece), PIECES[piece][2]
        wait_all(OFFSET + piece, off_recv.at[b], cut)
        received = off_recv[b, :, :, cut].astype(F32).reshape(DEVICES, COLS, ROWS, count)
        errors = []
        for d in range(COLS):
            offset = received[:, d].reshape(DEVICES * ROWS, count)
            error = (offset + mixed[d, :, cut]).astype(BF)
            hgrad[d, :, cut] = jnp.dot(lhalf[d], error, preferred_element_type=F32)
            if later:
                errors.append(error)
            else:
                step_left(piece, d, error)

        @pl.loop(0, DEVICES, unroll=16)
        def _(chunk):
            rows = pl.ds(pl.multiple_of(chunk * ROWS, ROWS), ROWS)
            left = jnp.concatenate([hgrad[d, rows, cut] for d in range(COLS)], axis=0).astype(BF)
            grad = jnp.dot(left, xg[b, chunk, cut, :], preferred_element_type=F32)
            rgrad[chunk] = rgrad[chunk] + jnp.where(on_block, grad, 0.0)

        return errors

    small_lane = lax.broadcasted_iota(jnp.int32, (COLS * ROWS, 128), 1)

    def take_right():
        @pl.loop(0, DEVICES, unroll=16)
        def _(chunk):
            value = right_recv[chunk].astype(F32)
            turned = pltpu.roll(value, 64, 1)
            half_low = small_lane[: COLS * ROWS // 2] < 64
            both = jnp.concatenate(
                [jnp.where(half_low, value, turned), jnp.where(half_low, turned, value)], axis=0
            )
            turned = pltpu.roll(both, 32, 1)
            even = jnp.where((small_lane & 63) < 32, both, turned)
            odd = jnp.where((small_lane & 63) < 32, turned, both)
            full = jnp.where(on_block, jnp.concatenate([even, even, odd, odd], axis=1), 0.0)
            rhalf[chunk] = (full - step_size * rgrad[chunk]).astype(BF)

    def give_output(piece):
        cut, count = span(piece), PIECES[piece][2]
        wait_all(MIXED + piece, mix_recv, cut)
        rows_in = mix_recv[:, :, cut].reshape(DEVICES * COLS * ROWS, count).astype(F32)
        mixed_rows = jnp.dot(rows_in.T.astype(BF), turn, preferred_element_type=F32)
        out[cut, :] = (base[cut, :] + mixed_rows).astype(BF)

    for sub in PIECE_SUBS[0]:
        along_z(sub, z, start)
        across(sub, z, start)

    block_id = lax.broadcasted_iota(jnp.int32, (64, 128), 0)
    lane_id = lax.broadcasted_iota(jnp.int32, (64, 128), 1)
    own_lane = block_id == 2 * (lane_id & 31) + ((lane_id >> 5) & 1)
    pairs = jnp.where(own_lane, 1.0, 0.0).astype(BF)
    spread = [
        jnp.dot(right_in[i].T.astype(BF), pairs, preferred_element_type=F32) for i in range(ROWS)
    ]
    spread = jnp.stack(spread, axis=1).reshape(DEVICES, COLS, ROWS, 128)
    low_lanes = lax.broadcasted_iota(jnp.int32, (DEVICES, COLS // 2, ROWS, 128), 3) < 64
    packed = jnp.where(low_lanes, spread[:, : COLS // 2], spread[:, COLS // 2 :])
    right_send[...] = packed.reshape(DEVICES, COLS * ROWS // 2, 128).astype(BF)
    lanes = slice(0, 128)
    send_all(RIGHT_IN, right_send, right_recv, lanes)

    xg[1, me] = jnp.dot(x2[...], split, preferred_element_type=F32).astype(BF)
    turn = jnp.where(
        col_id == ((row_id & (ROWS - 1)) * (width // ROWS)) + (row_id >> (ROWS.bit_length() - 1)), 1.0, 0.0
    ).astype(BF)
    rgrad[...] = jnp.zeros_like(rgrad)
    left_out[...] = left_in[...]
    take_left(left_in)
    clear(0)
    w_copy.wait()
    low = lax.broadcasted_iota(jnp.int32, (half, 128), 1) < 64

    @pl.loop(0, DEVICES)
    def _(chunk):
        rows = pl.ds(pl.multiple_of(chunk * half, half), half)
        for n in range(width // 128):
            first = w[rows, 256 * n : 256 * n + 128]
            second = w[rows, 256 * n + 128 : 256 * n + 256]
            lanes_n = slice(128 * n, 128 * n + 128)
            wd[chunk, :half, lanes_n] = jnp.concatenate([first[:, :64], second[:, :64]], axis=1)
            wd[chunk, half:, lanes_n] = jnp.concatenate([first[:, 64:], second[:, 64:]], axis=1)


    def early(piece, steps):
        def one(m, carry):
            apply_hidden(piece, z_order(m // 4) * 4 + lax.rem(x * 2 + lax.rem(m, 4), 4))
            return carry

        if steps > 0:
            lax.fori_loop(0, 4 * steps - 2, one, 0)

    gather_first(0, 2, False)
    wait_all(RIGHT_IN, right_recv, lanes)
    take_right()
    early(0, 2)
    gather_first(2, 4, True)
    finish_base(0, t1)
    clear(1)
    clear(2)
    mix(0)
    gather_rest(0, 3, False)
    backward(0, False)
    take_left(left_out)
    take_right()
    early(1, 3)
    early(2, 3 - LAG)
    gather_rest(3, 4, True)
    use_other(1, 3, True)
    finish_base(1, t2)
    mix(1)
    send_mixed(1)
    from_x(4, 3)
    use_other(2, 2, True)
    use_own(2, 3, True)
    use_other(2, 3, True)
    finish_base(2, t2)
    mix(2)
    send_mixed(2)
    backward(1, False)
    give_output(1)
    errors = backward(2, True)

    @pl.loop(0, DEVICES, unroll=16)
    def _(chunk):
        value = rgrad[chunk]
        folded = []
        for s in range(2):
            part = value[:, s * half : s * half + 128] + value[:, s * half + 128 : (s + 1) * half]
            part = part + pltpu.roll(part, 64, 1)
            folded.append(part + pltpu.roll(part, 32, 1))
        both = jnp.where((small_lane & 63) < 32, folded[0], folded[1])
        rows = COLS * ROWS // 2
        back_send[chunk] = jnp.where(small_lane[:rows] < 64, both[:rows], both[rows:]).astype(BF)

    send_all(RIGHT_BACK, back_send, back_recv, lanes)
    for d in range(COLS):
        step_left(2, d, errors[d])
    give_output(2)
    for sub in range(len(SUBS)):
        sent_gather(sub)
    for piece in range(len(PIECES)):
        b = PIECES[piece][0]
        sent_all(OFFSET + piece, off_send.at[b], off_recv.at[b], span(piece))
        if b == 1:
            sent_all(MIXED + piece, mix_send, mix_recv, span(piece))
    sent_all(RIGHT_IN, right_send, right_recv, lanes)
    wait_all(RIGHT_BACK, back_recv, lanes)
    returned = back_recv[...].astype(F32).reshape(DEVICES, COLS // 2, ROWS, 128)
    returned = jnp.concatenate(
        [jnp.where(low_lanes, returned, 0.0), jnp.where(low_lanes, 0.0, returned)], axis=1
    ).reshape(DEVICES * COLS, ROWS, 128)
    for i in range(ROWS):
        grad = lax.dot_general(
            pairs, returned[:, i, :].astype(BF), LANES, preferred_element_type=F32
        )
        right_out[i] = right_in[i] - step_size * grad

    sent_all(RIGHT_BACK, back_send, back_recv, lanes)


def hand_over(out, left, right, out_to, left_to, right_to):
    out_to[...] = out[...]
    left_to[...] = left[...]
    right_to[...] = right[...]


def fused_shards(
    x_first, target_first, x_second, target_second, frozen_weight_pairs, right_factor, left_factor
):
    tokens, width = x_first.shape
    step_size = 1.0 / tokens
    left_turned = jnp.swapaxes(left_factor, 1, 2)
    vmem = pl.BlockSpec(memory_space=pltpu.VMEM)
    slab = (DEVICES, COLS * ROWS, tokens)
    small = pltpu.VMEM((DEVICES, COLS * ROWS // 2, 128), BF)
    cols = pltpu.VMEM((COLS, DEVICES * ROWS, tokens), F32)
    square = pltpu.VMEM((COLS, 128, 128), BF)
    out, left_now, right_now = pl.pallas_call(
        functools.partial(adapter_kernel, step_size),
        out_shape=(
            jax.ShapeDtypeStruct((tokens, width), BF),
            jax.ShapeDtypeStruct(left_turned.shape, F32),
            jax.ShapeDtypeStruct(right_factor.shape, F32),
        ),
        in_specs=[vmem] * 4 + [pl.BlockSpec(memory_space=pl.ANY)] + [vmem] * 2,
        out_specs=(vmem, vmem, vmem),
        scratch_shapes=[
            pltpu.VMEM(frozen_weight_pairs.shape, BF),
            pltpu.VMEM((DEVICES, width, width), BF),
            pltpu.VMEM((2, DEVICES, tokens, width), BF),
            pltpu.VMEM((tokens, width), F32),
            pltpu.VMEM((tokens, width), F32),
            pltpu.VMEM((DEVICES, COLS * ROWS, width), F32),
            pltpu.VMEM((DEVICES, COLS * ROWS, width), BF),
            square,
            square,
            cols,
            cols,
            cols,
            small,
            small,
            small,
            small,
            pltpu.VMEM((2,) + slab, BF),
            pltpu.VMEM((2,) + slab, BF),
            pltpu.VMEM(slab, BF),
            pltpu.VMEM(slab, BF),
            pltpu.SemaphoreType.DMA,
            pltpu.SemaphoreType.DMA((len(SUBS), DEVICES, 4)),
            pltpu.SemaphoreType.DMA((len(SUBS), DEVICES)),
            pltpu.SemaphoreType.DMA((KINDS, DEVICES)),
            pltpu.SemaphoreType.DMA((KINDS, DEVICES)),
        ],
        compiler_params=pltpu.CompilerParams(
            collective_id=0, has_side_effects=True, vmem_limit_bytes=60 * 1024 * 1024
        ),
        name="adapter",
    )(
        x_first, target_first, x_second, target_second, frozen_weight_pairs, right_factor, left_turned
    )
    results = (out, left_now, right_now)
    out, left_now, right_now = pl.pallas_call(
        hand_over,
        out_shape=tuple(jax.ShapeDtypeStruct(a.shape, a.dtype) for a in results),
        in_specs=[vmem] * 3,
        out_specs=(vmem,) * 3,
        name="hand_over",
    )(*results)
    return (out, right_now, jnp.swapaxes(left_now, 1, 2))


def solution(mesh):
    fused = mesh.shape["tensor"] == DEVICES and mesh.shape["dp"] == 1
    body = fused_shards if fused else shards
    return jax.shard_map(
        body,
        mesh=mesh,
        in_specs=(
            P(("groups", "dp"), "tensor"),
            P(("groups", "dp"), "tensor"),
            P(("groups", "dp"), "tensor"),
            P(("groups", "dp"), "tensor"),
            P(None, "tensor"),
            P(("groups", "tensor"), None, None),
            P(("groups", "tensor"), None, None),
        ),
        out_specs=(
            P(("groups", "dp"), "tensor"),
            P(("groups", "tensor"), None, None),
            P(("groups", "tensor"), None, None),
        ),
        check_vma=False,
    )
```

```python
import functools

import jax
import jax.numpy as jnp
from jax import lax
from jax.experimental import pallas as pl
from jax.experimental.pallas import tpu as pltpu
from jax.sharding import PartitionSpec as P

MESH = pl.DeviceIdType.MESH
BF = jnp.bfloat16
F32 = jnp.float32
LANES = (((1,), (1,)), ((), ()))

exact_precision = lax.Precision.HIGHEST


def toward_blocks(buffer_rows):
    return lax.all_to_all(buffer_rows, "tensor", split_axis=0, concat_axis=1, tiled=True)


def toward_rows(buffer_blocks):
    return lax.all_to_all(buffer_blocks, "tensor", split_axis=1, concat_axis=0, tiled=True)


def rows_direct(buffer_rows):
    return lax.all_to_all(buffer_rows, "tensor", split_axis=0, concat_axis=1, tiled=True)


def blocks_direct(buffer_blocks):
    return lax.all_to_all(buffer_blocks, "tensor", split_axis=1, concat_axis=0, tiled=True)


def make_masks(rows_local, mesh_row_count, block_size):
    sub_count = mesh_row_count // block_size
    own_index = lax.axis_index("tensor") * rows_local + jnp.arange(rows_local, dtype=jnp.int32)
    positions = jnp.arange(sub_count, dtype=jnp.int32)
    block_mask = (positions[None, :] == (own_index % sub_count)[:, None]).astype(jnp.bfloat16)
    row_mask = (positions[:, None] == (own_index // block_size)[None, :]).astype(jnp.bfloat16)
    return (block_mask, row_mask)


def spread_rows(values, row_mask):
    block_size, rows_local, token_count = values.shape
    sub_count = row_mask.shape[0]
    spread = values[:, None, :, :] * row_mask[None, :, :, None]
    return spread.reshape(block_size * sub_count, rows_local, token_count)


def pick_block(received, block_mask):
    rows_local, mesh_row_count, token_count = received.shape
    sub_count = block_mask.shape[1]
    split = received.reshape(rows_local, sub_count, mesh_row_count // sub_count, token_count)
    return jnp.sum(split * block_mask[:, :, None, None], axis=1)


def spread_block(values, block_mask):
    rows_local, block_size, token_count = values.shape
    sub_count = block_mask.shape[1]
    spread = values[:, None, :, :] * block_mask[:, :, None, None]
    return spread.reshape(rows_local, sub_count * block_size, token_count)


def pick_rows(received, row_mask):
    mesh_row_count, rows_local, token_count = received.shape
    sub_count = row_mask.shape[0]
    split = received.reshape(mesh_row_count // sub_count, sub_count, rows_local, token_count)
    return jnp.sum(split * row_mask[None, :, :, None], axis=1)


def paired_product(segment, weight, block_size):
    token_count, width = segment.shape
    grid_local = weight.shape[1] // (2 * block_size)
    weight_rows = weight
    weight_rows = weight_rows.reshape(width // 2, grid_local, 2, block_size)
    pairs = segment.reshape(token_count, width // 2, 2)
    partial_value = jnp.einsum(
        "trs,rgsc->tgc", pairs, weight_rows, preferred_element_type=jnp.float32
    )
    return partial_value.reshape(token_count, grid_local * block_size)


def base_product(x_local, weight, block_size):
    return paired_product(lax.all_gather(x_local, "tensor", axis=1, tiled=True), weight, block_size)


def rows_to_block_side(values, masks_pair):
    return pick_block(rows_direct(spread_rows(values, masks_pair[1])), masks_pair[0])


def block_to_row_side(values, masks_pair):
    return pick_rows(blocks_direct(spread_block(values, masks_pair[0])), masks_pair[1])


def one_step(x_local, target, base_out, right_factor, left_factor, masks_pair, step_size):
    token_count = x_local.shape[0]
    rows_local = right_factor.shape[0]
    block_size = right_factor.shape[1]
    sub_count = left_factor.shape[1] // block_size
    upper_right_half = right_factor.astype(jnp.bfloat16)
    left_half = left_factor.astype(jnp.bfloat16)
    input_mesh_grid = x_local.reshape(token_count, rows_local, block_size)
    base_rows = base_out.reshape(token_count, rows_local, block_size).transpose(2, 1, 0)
    target_rows = (
        target.reshape(token_count, rows_local, block_size).transpose(2, 1, 0).astype(jnp.float32)
    )
    offset = (base_rows - target_rows).astype(jnp.bfloat16)
    hidden = jnp.einsum(
        "ves,esl->lev", input_mesh_grid, upper_right_half, preferred_element_type=jnp.float32
    ).astype(jnp.bfloat16)
    gathered = toward_blocks(jnp.repeat(hidden, sub_count, axis=0))
    mixed_out = jnp.einsum(
        "sit,sik->skt", gathered, left_half, preferred_element_type=jnp.float32
    ).astype(jnp.bfloat16)
    output_rows = None
    mixed_rows = block_to_row_side(mixed_out, masks_pair)
    output_rows = base_rows + mixed_rows.astype(jnp.float32)
    error_rows = (offset.astype(jnp.float32) + mixed_rows.astype(jnp.float32)).astype(jnp.bfloat16)
    error_blocks = rows_to_block_side(error_rows, masks_pair)
    left_grad = jnp.einsum(
        "sit,skt->sik", gathered, error_blocks, preferred_element_type=jnp.float32
    )
    back_terms = jnp.einsum(
        "skt,sik->sit", error_blocks, left_half, preferred_element_type=jnp.float32
    ).astype(jnp.bfloat16)
    returned = toward_rows(back_terms)
    hidden_gradient = jnp.sum(
        returned.reshape(block_size, sub_count, rows_local, token_count).astype(jnp.float32), axis=1
    )
    right_grad = jnp.einsum(
        "wfm,sfw->fms",
        input_mesh_grid.astype(jnp.float32),
        hidden_gradient,
        precision=exact_precision,
    )
    right_grad, left_grad = lax.psum((right_grad, left_grad), "dp")
    return (output_rows, right_factor - step_size * right_grad, left_factor - step_size * left_grad)


def shards(
    x_first, target_first, x_second, target_second, frozen_weight_pairs, right_factor, left_factor
):
    rows_local = right_factor.shape[0]
    block_size = right_factor.shape[1]
    token_count = x_first.shape[0]
    masks_pair = make_masks(rows_local, left_factor.shape[1], block_size)
    step_size = 1.0 / (token_count * lax.axis_size("dp"))
    base_first = base_product(x_first, frozen_weight_pairs, block_size)
    unused, right_now, left_now = one_step(
        x_first, target_first, base_first, right_factor, left_factor, masks_pair, step_size
    )
    base_second = base_product(x_second, frozen_weight_pairs, block_size)
    output_rows, right_now, left_now = one_step(
        x_second, target_second, base_second, right_now, left_now, masks_pair, step_size
    )
    result = (
        output_rows.transpose(2, 1, 0)
        .reshape(token_count, rows_local * block_size)
        .astype(jnp.bfloat16)
    )
    return (result, right_now, left_now)


Z_COUNT, DEVICES, ROWS, COLS = 4, 16, 8, 4
PIECES = ((0, 0, 384), (1, 0, 256), (1, 256, 128))
SUBS = ((0, 0, 192), (0, 192, 192), (1, 0, 128), (1, 128, 128), (1, 256, 128))
PIECE_SUBS = ((0, 1), (2, 3), (4,))
LAG = 1
RIGHT_IN, RIGHT_BACK, OFFSET, MIXED = 0, 1, 2, 2 + len(PIECES)
KINDS = 2 + 2 * len(PIECES)


def adapter_kernel(
    step_size, x1, t1_in, x2_in, t2_in, weight, right_from, left_from, out, left_out, right_out,
    t1, x2, t2, right_in, left_in, in_sem,
    w, wd, xg, acc, base, rgrad, rhalf, lhalf, lturn, hid, hgrad, mixed, right_send, right_recv,
    back_send, back_recv, off_send, off_recv, mix_send, mix_recv,
    w_sem, ag_send, ag_recv, a2a_send, a2a_recv,
):
    tokens, width = x1.shape
    half = width // 2
    me = lax.axis_index("tensor")
    z, x, core = me // 4, lax.rem(me // 2, 2), lax.rem(me, 2)
    x_peer = z * 4 + (1 - x) * 2 + core
    core_peer = z * 4 + x * 2 + (1 - core)

    w_copy = pltpu.make_async_copy(weight, w, w_sem)
    inputs = [
        pltpu.make_async_copy(source, target, in_sem.at[n])
        for n, (source, target) in enumerate(
            ((right_from, right_in), (left_from, left_in), (x2_in, x2), (t1_in, t1), (t2_in, t2))
        )
    ]
    for copy in inputs:
        copy.start()
    w_copy.start()

    barrier = pltpu.get_barrier_semaphore()

    @pl.loop(1, DEVICES)
    def _(n):
        pl.semaphore_signal(
            barrier, inc=1, device_id={"tensor": lax.rem(me + n, DEVICES)}, device_id_type=MESH
        )

    row_id = lax.broadcasted_iota(jnp.int32, (width, width), 0)
    col_id = lax.broadcasted_iota(jnp.int32, (width, width), 1)
    split = jnp.where(row_id == ((col_id & (half - 1)) << 1) + (col_id >> (half.bit_length() - 1)), 1.0, 0.0).astype(BF)
    xg[0, me] = jnp.dot(x1[...], split, preferred_element_type=F32).astype(BF)

    pl.semaphore_wait(barrier, DEVICES - 1)

    def exchange(kind, source, target, peer, cut):
        return pltpu.make_async_remote_copy(
            src_ref=source.at[peer, :, cut],
            dst_ref=target.at[me, :, cut],
            send_sem=a2a_send.at[kind, peer],
            recv_sem=a2a_recv.at[kind, me],
            device_id={"tensor": peer},
            device_id_type=MESH,
        )

    def landed(kind, target, peer, cut):
        return pltpu.make_async_remote_copy(
            src_ref=target.at[peer, :, cut],
            dst_ref=target.at[peer, :, cut],
            send_sem=a2a_send.at[kind, peer],
            recv_sem=a2a_recv.at[kind, peer],
            device_id={"tensor": peer},
            device_id_type=MESH,
        )

    def send_all(kind, source, target, cut):
        @pl.loop(1, DEVICES, unroll=5)
        def _(n):
            exchange(kind, source, target, lax.rem(me + n, DEVICES), cut).start()

        target[me, :, cut] = source[me, :, cut]

    def wait_all(kind, target, cut):
        @pl.loop(1, DEVICES, unroll=5)
        def _(n):
            landed(kind, target, lax.rem(me + n, DEVICES), cut).wait_recv()

    def sent_all(kind, source, target, cut):
        @pl.loop(1, DEVICES)
        def _(n):
            exchange(kind, source, target, lax.rem(me + n, DEVICES), cut).wait_send()

    def span(piece):
        return slice(PIECES[piece][1], PIECES[piece][1] + PIECES[piece][2])

    def hop(sub, chunk, direction, peer):
        b, first, count = SUBS[sub]
        return pltpu.make_async_remote_copy(
            src_ref=xg.at[b, chunk, first : first + count],
            dst_ref=xg.at[b, chunk, first : first + count],
            send_sem=ag_send.at[sub, chunk, direction],
            recv_sem=ag_recv.at[sub, chunk],
            device_id={"tensor": peer},
            device_id_type=MESH,
        )

    def z_order(k):
        high = z // 2
        mirrored = z * (1 - high) + (3 - z) * high
        order = k + (1 - k // 2) * mirrored * (1 - 2 * k)
        return order * (1 - high) + (3 - order) * high

    def along_z(sub, source_z, act):
        chunk = source_z * 4 + x * 2 + core

        @pl.when((source_z <= z) & (z < Z_COUNT - 1))
        def _():
            act(hop(sub, chunk, 0, me + 4))

        @pl.when((source_z >= z) & (z > 0))
        def _():
            act(hop(sub, chunk, 1, me - 4))

    def across(sub, source_z, act):
        chunk = source_z * 4 + x * 2 + core
        act(hop(sub, chunk, 2, x_peer))
        act(hop(sub, chunk, 3, core_peer))

    def start(copy):
        copy.start()

    def apply_base(piece, chunk):
        b, cut = PIECES[piece][0], span(piece)
        acc[cut, :] += jnp.dot(xg[b, chunk, cut, :], wd[chunk], preferred_element_type=F32)

    def apply_hidden(piece, chunk):
        b, cut = PIECES[piece][0], span(piece)
        value = lax.dot_general(
            rhalf[chunk], xg[b, chunk, cut, :], LANES, preferred_element_type=F32
        )
        for d in range(COLS):
            hid[d, pl.ds(pl.multiple_of(chunk * ROWS, ROWS), ROWS), cut] = value[
                d * ROWS : (d + 1) * ROWS
            ]

    def landed_all(piece, chunk):
        for sub in PIECE_SUBS[piece]:
            hop(sub, chunk, 3, core_peer).wait_recv()

    def use(piece, chunk, with_hidden):
        apply_base(piece, chunk)
        if with_hidden:
            apply_hidden(piece, chunk)

    def use_own(piece, k, with_hidden):
        def one(m, carry):
            chunk = z_order(k) * 4 + x * 2 + core + m * (1 - 2 * core)

            @pl.when(m > 0)
            def _():
                landed_all(piece, chunk)

            use(piece, chunk, with_hidden)
            return carry

        lax.fori_loop(0, 2, one, 0, unroll=True)

    def use_other(piece, k, with_hidden):
        def one(m, carry):
            chunk = z_order(k) * 4 + (1 - x) * 2 + core + m * (1 - 2 * core)

            @pl.when(m > 0)
            def _():
                landed_all(piece, chunk)

            use(piece, chunk, with_hidden)
            return carry

        lax.fori_loop(0, 2, one, 0, unroll=True)

    def from_z(sub, k):
        next_z = z_order(k)
        hop(sub, next_z * 4 + x * 2 + core, 3, core_peer).wait_recv()
        along_z(sub, next_z, start)
        across(sub, next_z, start)

    def from_x(sub, k):
        copy = hop(sub, z_order(k) * 4 + (1 - x) * 2 + core, 3, core_peer)
        copy.wait_recv()
        copy.start()

    def gather_first(first, last, with_hidden):
        def body(k, carry):
            @pl.when(k < 3)
            def _():
                from_z(0, k + 1)

            @pl.when(k == 3)
            def _():
                across(2, z, start)
                across(3, z, start)

            from_x(0, k)

            @pl.when(k < 3)
            def _():
                from_z(1, k + 1)

            @pl.when(k > 0)
            def _():
                use_other(0, k - 1, with_hidden)

            @pl.when(k == 2)
            def _():
                along_z(2, z, start)
                along_z(3, z, start)

            from_x(1, k)
            use_own(0, k, with_hidden)
            return carry

        lax.fori_loop(first, last, body, 0)
        if last == 4:
            use_other(0, 3, with_hidden)

    def gather_rest(first, last, with_hidden):
        def body(k, carry):
            @pl.when(k < 3)
            def _():
                from_z(2, k + 1)

            from_x(2, k)

            @pl.when(k < 3)
            def _():
                from_z(3, k + 1)

            @pl.when(k > 0)
            def _():
                use_other(1, k - 1, with_hidden)

            @pl.when(k == LAG - 1)
            def _():
                along_z(4, z, start)
                across(4, z, start)

            @pl.when(k >= LAG)
            def _():
                from_z(4, k - LAG + 1)

            from_x(3, k)
            use_own(1, k, with_hidden)

            @pl.when(k >= LAG)
            def _():
                from_x(4, k - LAG)

                @pl.when(k > LAG)
                def _():
                    use_other(2, k - LAG - 1, with_hidden)

                use_own(2, k - LAG, with_hidden)

            return carry

        lax.fori_loop(first, last, body, 0)

    def sent_gather(sub):
        @pl.loop(0, Z_COUNT)
        def _(source_z):
            along_z(sub, source_z, lambda copy: copy.wait_send())
            across(sub, source_z, lambda copy: copy.wait_send())
            hop(sub, source_z * 4 + (1 - x) * 2 + core, 3, core_peer).wait_send()

    def clear(piece):
        acc[span(piece), :] = jnp.zeros((PIECES[piece][2], width), F32)

    def finish_base(piece, target):
        b, cut, count = PIECES[piece][0], span(piece), PIECES[piece][2]
        value = acc[cut, :]
        if b == 1:
            base[cut, :] = value
        offset = (value - target[cut, :].astype(F32)).astype(BF)
        turned = lax.dot_general(turn, offset, LANES, preferred_element_type=F32)
        off_send[b, :, :, cut] = turned.astype(BF).reshape(DEVICES, COLS * ROWS, count)
        send_all(OFFSET + piece, off_send.at[b], off_recv.at[b], cut)

    def take_left(ref):
        for d in range(COLS):
            pair = jnp.concatenate([ref[2 * d], ref[2 * d + 1]], axis=0)
            lturn[d] = pair.astype(BF)
            lhalf[d] = pair.T.astype(BF)

    def mix(piece):
        cut = span(piece)
        for d in range(COLS):
            mixed[d, :, cut] = (
                jnp.dot(lturn[d], hid[d, :, cut].astype(BF), preferred_element_type=F32)
                .astype(BF)
                .astype(F32)
            )

    def send_mixed(piece):
        cut, count = span(piece), PIECES[piece][2]
        stacked = jnp.stack(
            [mixed[d, :, cut].reshape(DEVICES, ROWS, count) for d in range(COLS)], axis=1
        )
        mix_send[:, :, cut] = stacked.reshape(DEVICES, COLS * ROWS, count).astype(BF)
        send_all(MIXED + piece, mix_send, mix_recv, cut)

    block_row = lax.broadcasted_iota(jnp.int32, (COLS * ROWS, width), 0)
    block_col = lax.broadcasted_iota(jnp.int32, (COLS * ROWS, width), 1)
    on_block = lax.rem(block_row, ROWS) == lax.rem(block_col, half) // (half // ROWS)

    def step_left(piece, d, error):
        cut = span(piece)
        grad = step_size * lax.dot_general(
            error, hid[d, :, cut].astype(BF), LANES, preferred_element_type=F32
        )
        left_out[2 * d] = left_out[2 * d] - grad[:64]
        left_out[2 * d + 1] = left_out[2 * d + 1] - grad[64:]

    def backward(piece, later):
        b, cut, count = PIECES[piece][0], span(piece), PIECES[piece][2]
        wait_all(OFFSET + piece, off_recv.at[b], cut)
        received = off_recv[b, :, :, cut].astype(F32).reshape(DEVICES, COLS, ROWS, count)
        errors = []
        for d in range(COLS):
            offset = received[:, d].reshape(DEVICES * ROWS, count)
            error = (offset + mixed[d, :, cut]).astype(BF)
            hgrad[d, :, cut] = jnp.dot(lhalf[d], error, preferred_element_type=F32)
            if later:
                errors.append(error)
            else:
                step_left(piece, d, error)

        @pl.loop(0, DEVICES, unroll=16)
        def _(chunk):
            rows = pl.ds(pl.multiple_of(chunk * ROWS, ROWS), ROWS)
            left = jnp.concatenate([hgrad[d, rows, cut] for d in range(COLS)], axis=0).astype(BF)
            grad = jnp.dot(left, xg[b, chunk, cut, :], preferred_element_type=F32)
            rgrad[chunk] = rgrad[chunk] + jnp.where(on_block, grad, 0.0)

        return errors

    small_lane = lax.broadcasted_iota(jnp.int32, (COLS * ROWS, 128), 1)

    def take_right():
        @pl.loop(0, DEVICES, unroll=16)
        def _(chunk):
            value = right_recv[chunk].astype(F32)
            turned = pltpu.roll(value, 64, 1)
            half_low = small_lane[: COLS * ROWS // 2] < 64
            both = jnp.concatenate(
                [jnp.where(half_low, value, turned), jnp.where(half_low, turned, value)], axis=0
            )
            turned = pltpu.roll(both, 32, 1)
            even = jnp.where((small_lane & 63) < 32, both, turned)
            odd = jnp.where((small_lane & 63) < 32, turned, both)
            full = jnp.where(on_block, jnp.concatenate([even, even, odd, odd], axis=1), 0.0)
            rhalf[chunk] = (full - step_size * rgrad[chunk]).astype(BF)

    def give_output(piece):
        cut, count = span(piece), PIECES[piece][2]
        wait_all(MIXED + piece, mix_recv, cut)
        rows_in = mix_recv[:, :, cut].reshape(DEVICES * COLS * ROWS, count).astype(F32)
        mixed_rows = jnp.dot(rows_in.T.astype(BF), turn, preferred_element_type=F32)
        out[cut, :] = (base[cut, :] + mixed_rows).astype(BF)

    for sub in PIECE_SUBS[0]:
        along_z(sub, z, start)
        across(sub, z, start)

    for copy in inputs:
        copy.wait()
    block_id = lax.broadcasted_iota(jnp.int32, (64, 128), 0)
    lane_id = lax.broadcasted_iota(jnp.int32, (64, 128), 1)
    own_lane = block_id == 2 * (lane_id & 31) + ((lane_id >> 5) & 1)
    pairs = jnp.where(own_lane, 1.0, 0.0).astype(BF)
    spread = [
        jnp.dot(right_in[i].T.astype(BF), pairs, preferred_element_type=F32) for i in range(ROWS)
    ]
    spread = jnp.stack(spread, axis=1).reshape(DEVICES, COLS, ROWS, 128)
    low_lanes = lax.broadcasted_iota(jnp.int32, (DEVICES, COLS // 2, ROWS, 128), 3) < 64
    packed = jnp.where(low_lanes, spread[:, : COLS // 2], spread[:, COLS // 2 :])
    right_send[...] = packed.reshape(DEVICES, COLS * ROWS // 2, 128).astype(BF)
    lanes = slice(0, 128)
    send_all(RIGHT_IN, right_send, right_recv, lanes)

    xg[1, me] = jnp.dot(x2[...], split, preferred_element_type=F32).astype(BF)
    turn = jnp.where(
        col_id == ((row_id & (ROWS - 1)) * (width // ROWS)) + (row_id >> (ROWS.bit_length() - 1)), 1.0, 0.0
    ).astype(BF)
    rgrad[...] = jnp.zeros_like(rgrad)
    left_out[...] = left_in[...]
    take_left(left_in)
    clear(0)
    w_copy.wait()
    low = lax.broadcasted_iota(jnp.int32, (half, 128), 1) < 64

    @pl.loop(0, DEVICES)
    def _(chunk):
        rows = pl.ds(pl.multiple_of(chunk * half, half), half)
        for n in range(width // 128):
            first = w[rows, 256 * n : 256 * n + 128]
            second = w[rows, 256 * n + 128 : 256 * n + 256]
            lanes_n = slice(128 * n, 128 * n + 128)
            wd[chunk, :half, lanes_n] = jnp.concatenate([first[:, :64], second[:, :64]], axis=1)
            wd[chunk, half:, lanes_n] = jnp.concatenate([first[:, 64:], second[:, 64:]], axis=1)


    def early(piece, steps):
        def one(m, carry):
            apply_hidden(piece, z_order(m // 4) * 4 + lax.rem(x * 2 + lax.rem(m, 4), 4))
            return carry

        if steps > 0:
            lax.fori_loop(0, 4 * steps - 2, one, 0)

    gather_first(0, 2, False)
    wait_all(RIGHT_IN, right_recv, lanes)
    take_right()
    early(0, 2)
    gather_first(2, 4, True)
    finish_base(0, t1)
    clear(1)
    clear(2)
    mix(0)
    gather_rest(0, 3, False)
    backward(0, False)
    take_left(left_out)
    take_right()
    early(1, 3)
    early(2, 3 - LAG)
    gather_rest(3, 4, True)
    use_other(1, 3, True)
    finish_base(1, t2)
    mix(1)
    from_x(4, 3)
    use_other(2, 2, True)
    use_own(2, 3, True)
    use_other(2, 3, True)
    finish_base(2, t2)
    send_mixed(1)
    mix(2)
    send_mixed(2)
    backward(1, False)
    give_output(1)
    errors = backward(2, True)

    @pl.loop(0, DEVICES, unroll=16)
    def _(chunk):
        value = rgrad[chunk]
        folded = []
        for s in range(2):
            part = value[:, s * half : s * half + 128] + value[:, s * half + 128 : (s + 1) * half]
            part = part + pltpu.roll(part, 64, 1)
            folded.append(part + pltpu.roll(part, 32, 1))
        both = jnp.where((small_lane & 63) < 32, folded[0], folded[1])
        rows = COLS * ROWS // 2
        back_send[chunk] = jnp.where(small_lane[:rows] < 64, both[:rows], both[rows:]).astype(BF)

    send_all(RIGHT_BACK, back_send, back_recv, lanes)
    for d in range(COLS):
        step_left(2, d, errors[d])
    give_output(2)
    for sub in range(len(SUBS)):
        sent_gather(sub)
    for piece in range(len(PIECES)):
        b = PIECES[piece][0]
        sent_all(OFFSET + piece, off_send.at[b], off_recv.at[b], span(piece))
        if b == 1:
            sent_all(MIXED + piece, mix_send, mix_recv, span(piece))
    sent_all(RIGHT_IN, right_send, right_recv, lanes)
    wait_all(RIGHT_BACK, back_recv, lanes)
    returned = back_recv[...].astype(F32).reshape(DEVICES, COLS // 2, ROWS, 128)
    returned = jnp.concatenate(
        [jnp.where(low_lanes, returned, 0.0), jnp.where(low_lanes, 0.0, returned)], axis=1
    ).reshape(DEVICES * COLS, ROWS, 128)
    for i in range(ROWS):
        grad = lax.dot_general(
            pairs, returned[:, i, :].astype(BF), LANES, preferred_element_type=F32
        )
        right_out[i] = right_in[i] - step_size * grad

    sent_all(RIGHT_BACK, back_send, back_recv, lanes)


def hand_over(out, left, right, out_to, left_to, right_to, out_at, left_at, right_at, sems):
    arrays = ((out, out_at, out_to), (left, left_at, left_to), (right, right_at, right_to))
    loads = [pltpu.make_async_copy(a[0], a[1], sems.at[0, n]) for n, a in enumerate(arrays)]
    stores = [pltpu.make_async_copy(a[1], a[2], sems.at[1, n]) for n, a in enumerate(arrays)]
    for load in loads:
        load.start()
    for load, store in zip(loads, stores):
        load.wait()
        store.start()
    for store in stores:
        store.wait()


def fused_shards(
    x_first, target_first, x_second, target_second, frozen_weight_pairs, right_factor, left_factor
):
    tokens, width = x_first.shape
    step_size = 1.0 / tokens
    left_turned = jnp.swapaxes(left_factor, 1, 2)
    vmem = pl.BlockSpec(memory_space=pltpu.VMEM)
    slab = (DEVICES, COLS * ROWS, tokens)
    small = pltpu.VMEM((DEVICES, COLS * ROWS // 2, 128), BF)
    cols = pltpu.VMEM((COLS, DEVICES * ROWS, tokens), F32)
    square = pltpu.VMEM((COLS, 128, 128), BF)
    out, left_now, right_now = pl.pallas_call(
        functools.partial(adapter_kernel, step_size),
        out_shape=(
            jax.ShapeDtypeStruct((tokens, width), BF),
            jax.ShapeDtypeStruct(left_turned.shape, F32),
            jax.ShapeDtypeStruct(right_factor.shape, F32),
        ),
        in_specs=[vmem] + [pl.BlockSpec(memory_space=pl.ANY)] * 6,
        out_specs=(vmem, vmem, vmem),
        scratch_shapes=[
            pltpu.VMEM((tokens, width), BF),
            pltpu.VMEM((tokens, width), BF),
            pltpu.VMEM((tokens, width), BF),
            pltpu.VMEM(right_factor.shape, F32),
            pltpu.VMEM(left_turned.shape, F32),
            pltpu.SemaphoreType.DMA((5,)),
            pltpu.VMEM(frozen_weight_pairs.shape, BF),
            pltpu.VMEM((DEVICES, width, width), BF),
            pltpu.VMEM((2, DEVICES, tokens, width), BF),
            pltpu.VMEM((tokens, width), F32),
            pltpu.VMEM((tokens, width), F32),
            pltpu.VMEM((DEVICES, COLS * ROWS, width), F32),
            pltpu.VMEM((DEVICES, COLS * ROWS, width), BF),
            square,
            square,
            cols,
            cols,
            cols,
            small,
            small,
            small,
            small,
            pltpu.VMEM((2,) + slab, BF),
            pltpu.VMEM((2,) + slab, BF),
            pltpu.VMEM(slab, BF),
            pltpu.VMEM(slab, BF),
            pltpu.SemaphoreType.DMA,
            pltpu.SemaphoreType.DMA((len(SUBS), DEVICES, 4)),
            pltpu.SemaphoreType.DMA((len(SUBS), DEVICES)),
            pltpu.SemaphoreType.DMA((KINDS, DEVICES)),
            pltpu.SemaphoreType.DMA((KINDS, DEVICES)),
        ],
        compiler_params=pltpu.CompilerParams(
            collective_id=0, has_side_effects=True, vmem_limit_bytes=60 * 1024 * 1024
        ),
        name="adapter",
    )(
        x_first, target_first, x_second, target_second, frozen_weight_pairs, right_factor, left_turned
    )
    results = (out, left_now, right_now)
    anywhere = pl.BlockSpec(memory_space=pl.ANY)
    out, left_now, right_now = pl.pallas_call(
        hand_over,
        out_shape=tuple(jax.ShapeDtypeStruct(a.shape, a.dtype) for a in results),
        in_specs=[anywhere] * 3,
        out_specs=(anywhere,) * 3,
        scratch_shapes=[pltpu.VMEM(a.shape, a.dtype) for a in results]
        + [pltpu.SemaphoreType.DMA((2, 3))],
        name="hand_over",
    )(*results)
    return (out, right_now, jnp.swapaxes(left_now, 1, 2))


def solution(mesh):
    fused = mesh.shape["tensor"] == DEVICES and mesh.shape["dp"] == 1
    body = fused_shards if fused else shards
    return jax.shard_map(
        body,
        mesh=mesh,
        in_specs=(
            P(("groups", "dp"), "tensor"),
            P(("groups", "dp"), "tensor"),
            P(("groups", "dp"), "tensor"),
            P(("groups", "dp"), "tensor"),
            P(None, "tensor"),
            P(("groups", "tensor"), None, None),
            P(("groups", "tensor"), None, None),
        ),
        out_specs=(
            P(("groups", "dp"), "tensor"),
            P(("groups", "tensor"), None, None),
            P(("groups", "tensor"), None, None),
        ),
        check_vma=False,
    )
```
